512 devices in a mesh: grid: 16 (over y, core), dom: 32 (over z, x).
Axes of the slice: x: 4, y: 8, z: 8, core: 2. Of those that a mesh axis runs over, the one named last changes fastest.
Arguments:
- state: float32 [5, 125, 65536], P(None, None, ('grid', 'dom')), as said below
- inv_size: float32 [3, 65536], P(None, ('grid', 'dom')), may hold values from 1 to 4
- plus_order: int32 [3, 65536], P(None, ('grid', 'dom')), may hold values from 0 to 127, as said below
- minus_order: int32 [3, 65536], P(None, ('grid', 'dom')), may hold values from 0 to 127, as said below
- donor_cell: int32 [512, 1024], P(('grid', 'dom')), may hold values from 0 to 127
- donor_weights: float32 [512, 3, 5, 1024], P(('grid', 'dom')), as said below
- recv_slot: int32 [512, 600], P(('grid', 'dom')), may hold values from 0 to 1023, as said below
Outputs:
- rhs: float32 [5, 125, 65536], P(None, None, ('grid', 'dom'))
The draws below stay inside these ranges and needn't reach their ends.
Inputs may be any that keep to these rules, and one draw needn't show every extreme that they name: `plus_order`: within each device's block of 128 columns, every row is a permutation of the local element numbers. `minus_order`: within each device's block of 128 columns, every row is a permutation of the local element numbers. `state`: density lies in [0.9, 1.1], each momentum in [-0.1, 0.1], energy in [2.4, 2.6]. `donor_weights`: for each donor device, direction and slot, the five weights are the Lagrange basis of the five Gauss-Legendre points evaluated at one coordinate in [-0.8, 0.8]. `recv_slot`: entries of one device's row are distinct, and each names a slot whose source device (the slot // 2) lies in another grid than the row's device.
All inputs are finite; a program needn't handle non-finite values.
Results may differ from the reference program's by a relative error of at most 0.0003.
Values sent between devices are 32-bit elements; how exact they have to be, the bound alone decides.
A program may use at most 64 MiB of HBM per device.

```python
import math
import jax
import jax.numpy as jnp
from jax import lax

E_DEV = 128
FRP = 4
NGRIDS = 16
NPARTS = 32
DEVICE_TOTAL = 512
CAP = 1
REMOTE = 32
FRINGE_PTS = 600
SLOTS = 2
ELEMS = 65536


gauss_points = (-0.906179845938664, -0.5384693101056831, 0.0, 0.5384693101056831, 0.906179845938664)


def draw_state(key, part):
    uniform_part = jax.random.uniform(key, (5, 125, ELEMS), jnp.float32, -1.0, 1.0)
    centre = jnp.array([1.0, 0.0, 0.0, 0.0, 2.5], jnp.float32).reshape(5, 1, 1)
    return centre + 0.1 * uniform_part


def local_orders(key):
    key_list = jax.random.split(key, DEVICE_TOTAL * 3)
    orders = jax.vmap(lambda single: jax.random.permutation(single, E_DEV))(key_list)
    return jnp.transpose(orders.reshape(DEVICE_TOTAL, 3, E_DEV), (1, 0, 2)).reshape(3, DEVICE_TOTAL * E_DEV).astype(jnp.int32)


def draw_plus_order(key, part):
    return local_orders(jax.random.fold_in(key, 11))


def draw_minus_order(key, part):
    return local_orders(jax.random.fold_in(key, 23))


def draw_donor_weights(key, part):
    coordinate = jax.random.uniform(jax.random.fold_in(key, 31), (DEVICE_TOTAL, 3, 1, DEVICE_TOTAL * SLOTS), jnp.float32, -0.8, 0.8)
    basis = []
    for column in range(5):
        value = jnp.ones_like(coordinate)
        for other in range(5):
            if other != column:
                value = value * (coordinate - gauss_points[other]) / (gauss_points[column] - gauss_points[other])
        basis.append(value)
    return jnp.concatenate(basis, axis=2)


def draw_recv_slot(key, part):
    slot_total = DEVICE_TOTAL * SLOTS
    extra_score_key, ordering_key = jax.random.split(jax.random.fold_in(key, 37))
    extra_score = jax.random.randint(extra_score_key, (DEVICE_TOTAL,), 0, 4)
    extra_score = extra_score.at[0].set(5).at[DEVICE_TOTAL - 1].set(5)
    source_index = jnp.arange(slot_total, dtype=jnp.int32) // SLOTS
    order_keys = jax.random.split(ordering_key, DEVICE_TOTAL)
    rank_positions = jax.vmap(lambda single: jax.random.permutation(single, slot_total))(order_keys).astype(jnp.int32)
    receiver_grid = (jnp.arange(DEVICE_TOTAL, dtype=jnp.int32) // NPARTS)[:, None]
    permitted_mask = (source_index // NPARTS)[None, :] != receiver_grid
    score_values = jnp.where(permitted_mask, extra_score[source_index][None, :] * 1048576 + rank_positions, -1 - rank_positions)
    return jax.lax.top_k(score_values, FRINGE_PTS)[1].astype(jnp.int32)


def plant(values, rng, low, top_value):
    longest = values.shape.index(max(values.shape))
    spots = []
    for shift in (0, 1):
        where = [jax.random.randint(jax.random.fold_in(rng, axis), (), 0, length) for axis, length in enumerate(values.shape)]
        where[longest] = (where[longest] + shift) % values.shape[longest]
        spots.append(tuple(where))
    return values.at[spots[0]].set(low).at[spots[1]].set(top_value)


def shard_levels(key, extent, cuts, least, top_value):
    gain = 1.0
    for dim, shards_of in cuts:
        steps = jax.random.uniform(jax.random.fold_in(jax.random.fold_in(key, 6), dim), (shards_of,), jnp.float32, least / len(cuts), top_value / len(cuts))
        gain = gain * jnp.repeat(jnp.exp(steps), extent[dim] // shards_of).reshape((-1,) + (1,) * (len(extent) - 1 - dim))
    return gain


def setup_inputs(seed: int = 0) -> dict:
    streams_of = jax.random.split(jax.random.key(seed), 8)
    state = draw_state(jax.random.fold_in(streams_of[7], 71), 0)
    inv_size = jnp.clip(jnp.exp(math.log(4.0) - 1.3862944 * jax.random.uniform(streams_of[1], (3, ELEMS), jnp.float32) ** shard_levels(streams_of[1], (3, ELEMS), ((1, 512),), -0.2, 0.2)), 1.0, 4.0)
    plus_order = draw_plus_order(jax.random.fold_in(streams_of[7], 71), 0)
    minus_order = draw_minus_order(jax.random.fold_in(streams_of[7], 71), 0)
    donor_cell = plant(jax.random.randint(streams_of[4], (DEVICE_TOTAL, DEVICE_TOTAL * SLOTS), 0, E_DEV), jax.random.fold_in(streams_of[4], 1), 0, E_DEV - 1).astype(jnp.int32)
    donor_weights = draw_donor_weights(jax.random.fold_in(streams_of[7], 71), 0)
    recv_slot = draw_recv_slot(jax.random.fold_in(streams_of[7], 71), 0)
    return dict(state=state, inv_size=inv_size, plus_order=plus_order, minus_order=minus_order, donor_cell=donor_cell, donor_weights=donor_weights, recv_slot=recv_slot)


precise = lax.Precision.HIGHEST
volume_forms = ('ia,vabce->vibce', 'ib,vabce->vaice', 'ic,vabce->vabie')
face_forms = ('a,vabce->vbce', 'b,vabce->vace', 'c,vabce->vabe')
lift_forms = ('i,vbce->vibce', 'i,vace->vaice', 'i,vabe->vabie')

def gauss_nodes():
    outer = math.sqrt(5.0 + 2.0 * math.sqrt(10.0 / 7.0)) / 3.0
    inner = math.sqrt(5.0 - 2.0 * math.sqrt(10.0 / 7.0)) / 3.0
    return [-outer, -inner, 0.0, inner, outer]

def basis_value(nodes, column, target_positions):
    value = 1.0
    for other in range(5):
        if other != column:
            value = value * (target_positions - nodes[other]) / (nodes[column] - nodes[other])
    return value

def basis_slope(nodes, column, target_positions):
    total = 0.0
    for skipped in range(5):
        if skipped != column:
            value = 1.0 / (nodes[column] - nodes[skipped])
            for other in range(5):
                if other != column and other != skipped:
                    value = value * (target_positions - nodes[other]) / (nodes[column] - nodes[other])
            total = total + value
    return total

def legendre_slopes(target_positions):
    values = [1.0, target_positions]
    slopes = [0.0, 1.0]
    for order in range(1, 5):
        values.append(((2 * order + 1) * target_positions * values[order] - order * values[order - 1]) / (order + 1))
        slopes.append(slopes[order - 1] + (2 * order + 1) * values[order])
    return (slopes[4], slopes[5])

def tables():
    nodes = gauss_nodes()
    deriv = [[basis_slope(nodes, column, nodes[row]) for column in range(5)] for row in range(5)]
    lower = [basis_value(nodes, column, -1.0) for column in range(5)]
    upper = [basis_value(nodes, column, 1.0) for column in range(5)]
    lift_low = []
    lift_high = []
    for row in range(5):
        slope_four, slope_five = legendre_slopes(nodes[row])
        lift_low.append(-0.5 * (slope_five - slope_four))
        lift_high.append(0.5 * (slope_five + slope_four))
    return tuple((jnp.asarray(matrix, jnp.float32) for matrix in (deriv, lower, upper, lift_low, lift_high)))

def euler_flux(state, direction):
    density = state[0]
    momenta = state[1:4]
    energy = state[4]
    speed = momenta[direction] / density
    pressure = 0.4 * (energy - 0.5 * lax.optimization_barrier(jnp.sum(momenta * momenta, axis=0)) / density)
    pieces = [momenta[direction], momenta[0] * speed, momenta[1] * speed, momenta[2] * speed, (energy + pressure) * speed]
    pieces[1 + direction] = pieces[1 + direction] + pressure
    sound = jnp.sqrt(1.4 * pressure / density)
    return (jnp.stack(pieces), jnp.abs(speed) + sound)

def common_flux(left_state, right_state, direction):
    left_flux, left_wave = euler_flux(left_state, direction)
    right_flux, right_wave = euler_flux(right_state, direction)
    wave = jnp.maximum(left_wave, right_wave)
    return 0.5 * (left_flux + right_flux) - 0.5 * wave * (right_state - left_state)

def remote_fluxes(left_states, right_states):
    return jnp.stack([common_flux(left_states[direction], right_states[direction], direction) for direction in range(3)])

def slot_states(state, plus_rows, minus_rows):
    deriv, lower, upper, lift_low, lift_high = tables()
    columns = state.shape[-1]
    grid_form = state.reshape(5, 5, 5, 5, columns)
    high_slots = []
    low_slots = []
    for direction in range(3):
        high_face = jnp.einsum(face_forms[direction], upper, grid_form, precision=precise).reshape(5, 25, columns)
        low_face = jnp.einsum(face_forms[direction], lower, grid_form, precision=precise).reshape(5, 25, columns)
        high_slots.append(jnp.take(high_face, plus_rows[direction], axis=2))
        low_slots.append(jnp.take(low_face, minus_rows[direction], axis=2))
    return (jnp.stack(high_slots), jnp.stack(low_slots))

def interpolate(state, cells, weights, blocks):
    block_width = cells.shape[0] // blocks

    def one_block(index):
        block_cells = lax.dynamic_slice_in_dim(cells, index * block_width, block_width)
        block_weights = lax.dynamic_slice_in_dim(weights, index * block_width, block_width, axis=2)
        gathered = jnp.take(state, block_cells, axis=2).reshape(5, 5, 5, 5, block_width)
        reduced = jnp.einsum('as,vabcs->vbcs', block_weights[0], gathered, precision=precise)
        reduced = jnp.einsum('bs,vbcs->vcs', block_weights[1], reduced, precision=precise)
        return jnp.einsum('cs,vcs->vs', block_weights[2], reduced, precision=precise)
    values = lax.map(one_block, jnp.arange(blocks, dtype=jnp.int32))
    return jnp.transpose(values, (1, 0, 2)).reshape(5, blocks * block_width)

def assemble(high_slots, low_slots, remote_plus, remote_minus, fringe, plus_rows, minus_rows):
    remote = remote_plus.shape[-1]
    start = remote + fringe.shape[-1]
    plus_parts = []
    minus_parts = []
    for direction in range(3):
        local_flux = common_flux(high_slots[direction][:, :, start:], low_slots[direction][:, :, start:], direction)
        fringe_high = common_flux(high_slots[direction][:, :, remote:start], fringe[direction, 1], direction)
        fringe_low = common_flux(fringe[direction, 0], low_slots[direction][:, :, remote:start], direction)
        plus_slots = jnp.concatenate([remote_plus[direction], fringe_high, local_flux], axis=2)
        minus_slots = jnp.concatenate([remote_minus[direction], fringe_low, local_flux], axis=2)
        plus_parts.append(jnp.zeros_like(plus_slots).at[:, :, plus_rows[direction]].set(plus_slots))
        minus_parts.append(jnp.zeros_like(minus_slots).at[:, :, minus_rows[direction]].set(minus_slots))
    return (jnp.stack(plus_parts), jnp.stack(minus_parts))

def divergence(state, scales, plus_common, minus_common):
    deriv, lower, upper, lift_low, lift_high = tables()
    columns = state.shape[-1]
    grid_form = state.reshape(5, 5, 5, 5, columns)
    total = jnp.zeros_like(grid_form)
    for direction in range(3):
        flux = euler_flux(grid_form, direction)[0]
        inner = jnp.einsum(volume_forms[direction], deriv, flux, precision=precise)
        low_jump = minus_common[direction].reshape(5, 5, 5, columns) - jnp.einsum(face_forms[direction], lower, flux, precision=precise)
        high_jump = plus_common[direction].reshape(5, 5, 5, columns) - jnp.einsum(face_forms[direction], upper, flux, precision=precise)
        inner = inner + jnp.einsum(lift_forms[direction], lift_low, low_jump, precision=precise)
        inner = inner + jnp.einsum(lift_forms[direction], lift_high, high_jump, precision=precise)
        total = total + scales[direction] * inner
    return (-total).reshape(5, 125, columns)

def reference(state, inv_size, plus_order, minus_order, donor_cell, donor_weights, recv_slot):

    def gather_side(index):
        offset = index.astype(jnp.int32) * E_DEV
        block = lax.dynamic_slice_in_dim(state, offset, E_DEV, axis=2)
        plus_rows = lax.dynamic_slice_in_dim(plus_order, offset, E_DEV, axis=1)
        minus_rows = lax.dynamic_slice_in_dim(minus_order, offset, E_DEV, axis=1)
        high_slots, low_slots = slot_states(block, plus_rows, minus_rows)
        values = interpolate(block, donor_cell[index], donor_weights[index], NGRIDS)
        return (high_slots[..., :REMOTE], low_slots[..., :REMOTE], values)
    sent_high, sent_low, donor_values = lax.map(gather_side, jnp.arange(DEVICE_TOTAL, dtype=jnp.int32))

    def regroup(sent):
        shaped = sent.reshape(NGRIDS, NPARTS, 3, 5, 25, NPARTS, CAP)
        return jnp.transpose(shaped, (0, 5, 2, 3, 4, 1, 6)).reshape(DEVICE_TOTAL, 3, 5, 25, REMOTE)
    partner_high = regroup(sent_high)
    partner_low = regroup(sent_low)
    arrived = jnp.transpose(donor_values.reshape(DEVICE_TOTAL, 5, DEVICE_TOTAL, SLOTS), (2, 1, 0, 3)).reshape(DEVICE_TOTAL, 5, DEVICE_TOTAL * SLOTS)

    def finish(index, result):
        index = index.astype(jnp.int32)
        offset = index * E_DEV
        block = lax.dynamic_slice_in_dim(state, offset, E_DEV, axis=2)
        scales = lax.dynamic_slice_in_dim(inv_size, offset, E_DEV, axis=1)
        plus_rows = lax.dynamic_slice_in_dim(plus_order, offset, E_DEV, axis=1)
        minus_rows = lax.dynamic_slice_in_dim(minus_order, offset, E_DEV, axis=1)
        high_slots, low_slots = slot_states(block, plus_rows, minus_rows)
        fringe = jnp.take(arrived[index], recv_slot[index], axis=1)
        fringe = jnp.transpose(fringe.reshape(5, 3, 2, 25, FRP), (1, 2, 0, 3, 4))
        remote_plus = remote_fluxes(high_slots[..., :REMOTE], partner_low[index])
        remote_minus = remote_fluxes(partner_high[index], low_slots[..., :REMOTE])
        plus_common, minus_common = assemble(high_slots, low_slots, remote_plus, remote_minus, fringe, plus_rows, minus_rows)
        rhs_block = divergence(block, scales, plus_common, minus_common)
        return lax.dynamic_update_slice_in_dim(result, rhs_block, offset, axis=2)
    result = jnp.zeros((5, 125, DEVICE_TOTAL * E_DEV), jnp.float32)
    return lax.fori_loop(0, DEVICE_TOTAL, finish, result)
```

```python
import functools
import math

import jax
import jax.numpy as jnp
import numpy as np
from jax import lax
from jax.experimental import pallas as pl
from jax.experimental.pallas import tpu as pltpu
from jax.sharding import PartitionSpec as P

MESH = pl.DeviceIdType.MESH
LANES = 128
ROWS = 32
FRP = 4


def gauss_nodes():
    outer = math.sqrt(5.0 + 2.0 * math.sqrt(10.0 / 7.0)) / 3.0
    inner = math.sqrt(5.0 - 2.0 * math.sqrt(10.0 / 7.0)) / 3.0
    return [-outer, -inner, 0.0, inner, outer]


def basis_value(nodes, column, x):
    value = 1.0
    for other in range(5):
        if other != column:
            value = value * (x - nodes[other]) / (nodes[column] - nodes[other])
    return value


def basis_slope(nodes, column, x):
    total = 0.0
    for skipped in range(5):
        if skipped != column:
            value = 1.0 / (nodes[column] - nodes[skipped])
            for other in range(5):
                if other != column and other != skipped:
                    value = value * (x - nodes[other]) / (nodes[column] - nodes[other])
            total = total + value
    return total


def legendre_slopes(x):
    values = [1.0, x]
    slopes = [0.0, 1.0]
    for order in range(1, 5):
        values.append(((2 * order + 1) * x * values[order] - order * values[order - 1]) / (order + 1))
        slopes.append(slopes[order - 1] + (2 * order + 1) * values[order])
    return slopes[4], slopes[5]


def split_point(p, direction):
    index = [p // 25, p // 5 % 5, p % 5]
    along = index.pop(direction)
    return along, 5 * index[0] + index[1]


def matrices():
    nodes = gauss_nodes()
    deriv = np.array([[basis_slope(nodes, m, x) for m in range(5)] for x in nodes])
    lower = np.array([basis_value(nodes, m, -1.0) for m in range(5)])
    upper = np.array([basis_value(nodes, m, 1.0) for m in range(5)])
    slopes = [legendre_slopes(x) for x in nodes]
    lift_low = np.array([-0.5 * (five - four) for four, five in slopes])
    lift_high = np.array([0.5 * (five + four) for four, five in slopes])
    folded = deriv - np.outer(lift_low, lower) - np.outer(lift_high, upper)
    faces = np.zeros((2, 3, ROWS, LANES))
    volume = np.zeros((LANES, 3, LANES))
    lift = np.zeros((LANES, 2, 3, ROWS))
    for direction in range(3):
        for p in range(125):
            i, t = split_point(p, direction)
            faces[0, direction, t, p] = upper[i]
            faces[1, direction, t, p] = lower[i]
            lift[p, 0, direction, t] = -lift_high[i]
            lift[p, 1, direction, t] = -lift_low[i]
            for other in range(125):
                m, s = split_point(other, direction)
                if s == t:
                    volume[p, direction, other] = -folded[i, m]
    faces[:, :, 25:] = faces[:, :, :1]
    return (
        jnp.asarray(faces.reshape(6 * ROWS, LANES), jnp.float32),
        jnp.asarray(volume.reshape(LANES, 3 * LANES), jnp.float32),
        jnp.asarray(lift.reshape(LANES, 6 * ROWS), jnp.float32),
    )


def lane_take(x, index):
    return jnp.take_along_axis(x, index, axis=1, mode="promise_in_bounds")


def spread(row, rows):
    return jnp.broadcast_to(row, (rows, row.shape[-1]))


def matmul(a, b):
    return jnp.dot(a, b, precision=lax.Precision.HIGH, preferred_element_type=jnp.float32)


def euler(w, direction):
    rho, momenta, energy = w[0], w[1:4], w[4]
    inverse = 1.0 / rho
    speed = momenta[direction] * inverse
    square = momenta[0] * momenta[0] + momenta[1] * momenta[1] + momenta[2] * momenta[2]
    pressure = 0.4 * (energy - 0.5 * square * inverse)
    flux = [momenta[direction]] + [m * speed for m in momenta] + [(energy + pressure) * speed]
    flux[1 + direction] = flux[1 + direction] + pressure
    return flux, speed, pressure * inverse


def common(left, right, direction):
    left_flux, left_speed, left_ratio = euler(left, direction)
    right_flux, right_speed, right_ratio = euler(right, direction)
    wave = jnp.maximum(
        jnp.abs(left_speed) + jnp.sqrt(1.4 * left_ratio),
        jnp.abs(right_speed) + jnp.sqrt(1.4 * right_ratio),
    )
    return [
        0.5 * (lf + rf) - 0.5 * wave * (r - l)
        for lf, rf, l, r in zip(left_flux, right_flux, left, right)
    ]


def load_state(state_ref, points):
    for v in range(5):
        points[v, 0:120, :] = state_ref[v, 0:120, :]
        points[v, 120:125, :] = state_ref[v, 120:125, :]
        points[v, 125:128, :] = state_ref[v, 122:125, :]


def donor_values(points, cell_ref, weight_ref, pair_weight, weight, donor_ref):
    slots = cell_ref.shape[-1]
    grids = donor_ref.shape[0]
    width = slots // grids
    weight[120:128, :] = jnp.zeros((8, slots), jnp.float32)
    for b in range(5):
        pair_weight[5 * b : 5 * b + 5, :] = weight_ref[0, 1, b : b + 1, :] * weight_ref[0, 2, :, :]
    for a in range(5):
        weight[25 * a : 25 * a + 25, :] = weight_ref[0, 0, a : a + 1, :] * pair_weight[0:25, :]
    for tile in range(slots // LANES):
        lanes = slice(tile * LANES, (tile + 1) * LANES)
        index = spread(cell_ref[0:1, lanes], LANES)
        scale = weight[:, lanes]
        for v in range(5):
            picked = lane_take(points[v], index)
            row = jnp.sum(picked * scale, axis=0, keepdims=True)
            donor_ref[tile * (LANES // width), v : v + 1, :] = row
        first = tile * (LANES // width)
        for k in range(1, LANES // width):
            donor_ref[first + k, :, :] = pltpu.roll(donor_ref[first], LANES - k * width, axis=1)


def face_slots(points, plus_ref, minus_ref, face_matrix, slot_ref):
    for v in range(5):
        faces = matmul(face_matrix, points[v])
        for side, order in ((0, plus_ref), (1, minus_ref)):
            for d in range(3):
                start = (side * 3 + d) * ROWS
                slot_ref[side, d, v] = lane_take(
                    faces[start : start + ROWS], spread(order[d : d + 1, :], ROWS)
                )


def face_messages(slot_ref, message_ref):
    count = message_ref.shape[0]
    for row in range(8):
        columns = [
            slot_ref[n // 15, n // 5 % 3, n % 5] for n in range(4 * row, min(4 * row + 4, 30))
        ]
        columns += [columns[-1]] * (4 - len(columns))
        message_ref[:, row, :] = jnp.concatenate(columns, axis=0).T[0:count]


def local_kernel(
    state_ref, plus_ref, minus_ref, cell_ref, weight_ref, face_ref,
    donor_ref, slot_ref, message_ref, points, pair_weight, weight,
):
    load_state(state_ref, points)
    donor_values(points, cell_ref, weight_ref, pair_weight, weight, donor_ref)
    face_slots(points, plus_ref, minus_ref, face_ref[...], slot_ref)
    face_messages(slot_ref, message_ref)


def ring_distance(offset, size):
    return min(offset, size - offset)


def exchange_kernel(
    grids, parts, donor_ref, message_ref, partner_ref, arrived_ref,
    gathered, relay, sends, recvs,
):
    grid = lax.axis_index("grid")
    part = lax.axis_index("dom")
    across = 4 if parts % 4 == 0 else 1
    down = parts // across

    def part_at(offset):
        z, x = offset // across, offset % across
        return lax.rem(part // across + z, down) * across + lax.rem(lax.rem(part, across) + x, across)

    grid_steps = sorted(range(1, grids), key=lambda k: -ring_distance(k, grids))
    part_steps = sorted(
        range(1, parts),
        key=lambda k: -(ring_distance(k // across, down) + ring_distance(k % across, across)),
    )
    barrier = pltpu.get_barrier_semaphore()
    for k in part_steps:
        pl.semaphore_signal(barrier, inc=1, device_id=(grid, part_at(k)), device_id_type=MESH)
    for k in grid_steps:
        pl.semaphore_signal(
            barrier, inc=1, device_id=(lax.rem(grid + k, grids), part), device_id_type=MESH
        )
    pl.semaphore_wait(barrier, grids + parts - 2)

    def to_grid(k):
        peer = lax.rem(grid + k, grids)
        return pltpu.make_async_remote_copy(
            src_ref=donor_ref.at[peer], dst_ref=gathered.at[grid],
            send_sem=sends.at[k - 1], recv_sem=recvs.at[k - 1],
            device_id=(peer, part), device_id_type=MESH,
        )

    def to_part(k, source, target, base):
        peer = part_at(k)
        return pltpu.make_async_remote_copy(
            src_ref=source.at[peer], dst_ref=target.at[part],
            send_sem=sends.at[base + k - 1], recv_sem=recvs.at[base + k - 1],
            device_id=(grid, peer), device_id_type=MESH,
        )

    first = [to_grid(k) for k in grid_steps]
    faces = [to_part(k, message_ref, partner_ref, grids - 1) for k in part_steps]
    second = [to_part(k, relay, arrived_ref, grids + parts - 2) for k in part_steps]
    for copy in first:
        copy.start()
    for copy in faces:
        copy.start()
    gathered[grid] = donor_ref[grid]
    partner_ref[part] = message_ref[part]
    for copy in first:
        copy.wait_recv()
    width = gathered.shape[2]
    turned = gathered[...].reshape(grids * 8, width)
    if grids * 8 < LANES:
        turned = jnp.concatenate([turned] * (LANES // (grids * 8)), axis=0)
    turned = turned.T
    relay[...] = turned[0 : relay.shape[0] * relay.shape[1]].reshape(relay.shape)
    for copy in second:
        copy.start()
    arrived_ref[part] = relay[part]
    for copy in faces:
        copy.wait_recv()
    for copy in second:
        copy.wait_recv()
    for copy in first + faces + second:
        copy.wait_send()


def fringe_values(arrived_ref, pick_ref, by_grid, fringe):
    parts, slots, width = arrived_ref.shape
    grids = by_grid.shape[0]
    each = parts * slots
    turned = arrived_ref[...].reshape(each, width)
    turned = jnp.concatenate([turned] * (LANES // each), axis=0).T
    by_grid[...] = turned[0 : grids * 8].reshape(grids, 8, LANES)
    for k in range(6):
        pick = spread(pick_ref[k : k + 1, :], 8)
        owner, place = pick // each, lax.rem(pick, each)
        value = lane_take(by_grid[0], place)
        for g in range(1, grids):
            value = jnp.where(owner == g, lane_take(by_grid[g], place), value)
        fringe[k] = value


def finish_kernel(
    remote, state_ref, scale_ref, plus_ref, minus_ref, pick_ref, slot_ref, partner_ref, arrived_ref,
    volume_ref, lift_ref, out_ref, points, by_grid, fringe, partner, flux, jump,
):
    load_state(state_ref, points)
    w = [points[v] for v in range(5)]
    for d in range(3):
        pieces = euler(w, d)[0]
        for v in range(5):
            flux[v, d * LANES : (d + 1) * LANES, :] = pieces[v] * spread(scale_ref[d : d + 1, :], LANES)

    for row in range(8):
        block = partner_ref[:, row, :]
        block = jnp.concatenate([block] * (LANES // remote), axis=0).T
        partner[row * LANES : (row + 1) * LANES, :] = block
    fringe_values(arrived_ref, pick_ref, by_grid, fringe)

    lane = lax.broadcasted_iota(jnp.int32, (ROWS, LANES), 1)
    point = lax.broadcasted_iota(jnp.int32, (ROWS, LANES), 0)
    point = jnp.where(point < 25, point, 0)
    place = jnp.clip(FRP * point + lane - remote, 0, LANES - 1)
    shared, outer = lane < remote, lane < remote + FRP
    element = lax.broadcasted_iota(jnp.int32, (LANES, LANES), 0)
    count = lax.broadcasted_iota(jnp.int32, (8, LANES), 1).astype(jnp.bfloat16)

    def inverse(order):
        chosen = (element == spread(order, LANES)).astype(jnp.float32).astype(jnp.bfloat16)
        slots = lax.dot_general(
            count, chosen, (((1,), (1,)), ((), ())), preferred_element_type=jnp.float32
        )
        return spread(slots[0:1].astype(jnp.int32), ROWS)

    def other(side, d, v, own):
        start = ((side * 3 + d) * 5 + v) * ROWS
        edge = lane_take(spread(fringe[2 * d + side, v : v + 1, :], ROWS), place)
        return jnp.where(shared, partner[start : start + ROWS, :], jnp.where(outer, edge, own))

    for d in range(3):
        high = [slot_ref[0, d, v] for v in range(5)]
        low = [slot_ref[1, d, v] for v in range(5)]
        right = [other(1, d, v, low[v]) for v in range(5)]
        left = [other(0, d, v, high[v]) for v in range(5)]
        scale = spread(scale_ref[d : d + 1, :], ROWS)
        for side, order, value in (
            (0, plus_ref, common(high, right, d)),
            (1, minus_ref, common(left, low, d)),
        ):
            back = inverse(order[d : d + 1, :])
            start = (side * 3 + d) * ROWS
            for v in range(5):
                jump[v, start : start + ROWS, :] = lane_take(value[v], back) * scale
    for v in range(5):
        total = matmul(volume_ref[...], flux[v]) + matmul(lift_ref[...], jump[v])
        out_ref[v] = total[0:125]


def body(grids, parts, state, scales, plus, minus, cell, weights, picks):
    vmem = pl.BlockSpec(memory_space=pltpu.VMEM)
    f32 = jnp.float32
    slots = cell.shape[-1] // (grids * parts)
    face_matrix, volume, lift = matrices()
    donors, own, messages = pl.pallas_call(
        local_kernel,
        out_shape=(
            jax.ShapeDtypeStruct((grids, 8, LANES), f32),
            jax.ShapeDtypeStruct((2, 3, 5, ROWS, LANES), f32),
            jax.ShapeDtypeStruct((parts, 8, LANES), f32),
        ),
        in_specs=[vmem] * 6,
        out_specs=(vmem,) * 3,
        scratch_shapes=[
            pltpu.VMEM((5, LANES, LANES), f32),
            pltpu.VMEM((32, cell.shape[-1]), f32),
            pltpu.VMEM((LANES, cell.shape[-1]), f32),
        ],
        name="local",
    )(state, plus, minus, cell, weights, face_matrix)

    copies = grids - 1 + 2 * (parts - 1)
    partner, arrived = pl.pallas_call(
        functools.partial(exchange_kernel, grids, parts),
        out_shape=(
            jax.ShapeDtypeStruct((parts, 8, LANES), f32),
            jax.ShapeDtypeStruct((parts, slots, LANES), f32),
        ),
        in_specs=[vmem] * 2,
        out_specs=(vmem,) * 2,
        scratch_shapes=[
            pltpu.VMEM((grids, 8, LANES), f32),
            pltpu.VMEM((parts, slots, LANES), f32),
            pltpu.SemaphoreType.DMA((copies,)),
            pltpu.SemaphoreType.DMA((copies,)),
        ],
        compiler_params=pltpu.CompilerParams(collective_id=0, has_side_effects=True),
        name="exchange",
    )(donors, messages)

    picks = jnp.pad(picks.reshape(6, 25 * FRP), ((0, 0), (0, LANES - 25 * FRP)))
    return pl.pallas_call(
        functools.partial(finish_kernel, parts),
        out_shape=jax.ShapeDtypeStruct(state.shape, f32),
        in_specs=[vmem] * 10,
        out_specs=vmem,
        scratch_shapes=[
            pltpu.VMEM((5, LANES, LANES), f32),
            pltpu.VMEM((grids, 8, LANES), f32),
            pltpu.VMEM((6, 8, LANES), f32),
            pltpu.VMEM((8 * LANES, LANES), f32),
            pltpu.VMEM((5, 3 * LANES, LANES), f32),
            pltpu.VMEM((5, 6 * ROWS, LANES), f32),
        ],
        name="finish",
    )(state, scales, plus, minus, picks, own, partner, arrived, volume, lift)


def solution(mesh):
    both = ("grid", "dom")
    return jax.shard_map(
        functools.partial(body, mesh.shape["grid"], mesh.shape["dom"]),
        mesh=mesh,
        in_specs=(
            P(None, None, both),
            P(None, both),
            P(None, both),
            P(None, both),
            P(both, None),
            P(both, None, None, None),
            P(both, None),
        ),
        out_specs=P(None, None, both),
        check_vma=False,
    )
```

```python
import functools
import math

import jax
import jax.numpy as jnp
import numpy as np
from jax import lax
from jax.experimental import pallas as pl
from jax.experimental.pallas import tpu as pltpu
from jax.sharding import PartitionSpec as P

MESH = pl.DeviceIdType.MESH
LANES = 128
ROWS = 32
FRP = 4


def gauss_nodes():
    outer = math.sqrt(5.0 + 2.0 * math.sqrt(10.0 / 7.0)) / 3.0
    inner = math.sqrt(5.0 - 2.0 * math.sqrt(10.0 / 7.0)) / 3.0
    return [-outer, -inner, 0.0, inner, outer]


def basis_value(nodes, column, x):
    value = 1.0
    for other in range(5):
        if other != column:
            value = value * (x - nodes[other]) / (nodes[column] - nodes[other])
    return value


def basis_slope(nodes, column, x):
    total = 0.0
    for skipped in range(5):
        if skipped != column:
            value = 1.0 / (nodes[column] - nodes[skipped])
            for other in range(5):
                if other != column and other != skipped:
                    value = value * (x - nodes[other]) / (nodes[column] - nodes[other])
            total = total + value
    return total


def legendre_slopes(x):
    values = [1.0, x]
    slopes = [0.0, 1.0]
    for order in range(1, 5):
        values.append(((2 * order + 1) * x * values[order] - order * values[order - 1]) / (order + 1))
        slopes.append(slopes[order - 1] + (2 * order + 1) * values[order])
    return slopes[4], slopes[5]


def split_point(p, direction):
    index = [p // 25, p // 5 % 5, p % 5]
    along = index.pop(direction)
    return along, 5 * index[0] + index[1]


def matrices():
    nodes = gauss_nodes()
    deriv = np.array([[basis_slope(nodes, m, x) for m in range(5)] for x in nodes])
    lower = np.array([basis_value(nodes, m, -1.0) for m in range(5)])
    upper = np.array([basis_value(nodes, m, 1.0) for m in range(5)])
    slopes = [legendre_slopes(x) for x in nodes]
    lift_low = np.array([-0.5 * (five - four) for four, five in slopes])
    lift_high = np.array([0.5 * (five + four) for four, five in slopes])
    folded = deriv - np.outer(lift_low, lower) - np.outer(lift_high, upper)
    faces = np.zeros((2, 3, ROWS, LANES))
    volume = np.zeros((LANES, 3, LANES))
    lift = np.zeros((LANES, 2, 3, ROWS))
    for direction in range(3):
        for p in range(125):
            i, t = split_point(p, direction)
            faces[0, direction, t, p] = upper[i]
            faces[1, direction, t, p] = lower[i]
            lift[p, 0, direction, t] = -lift_high[i]
            lift[p, 1, direction, t] = -lift_low[i]
            for other in range(125):
                m, s = split_point(other, direction)
                if s == t:
                    volume[p, direction, other] = -folded[i, m]
    faces[:, :, 25:] = faces[:, :, :1]
    return (
        jnp.asarray(faces.reshape(6 * ROWS, LANES), jnp.float32),
        jnp.asarray(volume.reshape(LANES, 3 * LANES), jnp.float32),
        jnp.asarray(lift.reshape(LANES, 6 * ROWS), jnp.float32),
    )


def lane_take(x, index):
    return jnp.take_along_axis(x, index, axis=1, mode="promise_in_bounds")


def spread(row, rows):
    return jnp.broadcast_to(row, (rows, row.shape[-1]))


def matmul(a, b):
    return jnp.dot(a, b, precision=lax.Precision.HIGH, preferred_element_type=jnp.float32)


def pressure_of(w, inverse):
    square = w[1] * w[1] + w[2] * w[2] + w[3] * w[3]
    return 0.4 * (w[4] - 0.5 * square * inverse)


def euler(w, direction):
    inverse = 1.0 / w[0]
    speed = w[1 + direction] * inverse
    pressure = pressure_of(w, inverse)
    flux = [w[1 + direction]] + [m * speed for m in w[1:4]] + [(w[4] + pressure) * speed]
    flux[1 + direction] = flux[1 + direction] + (pressure - 1.0)
    return flux, jnp.abs(speed) + jnp.sqrt(1.4 * pressure * inverse)


def common(left, right, direction):
    left_flux, left_wave = euler(left, direction)
    right_flux, right_wave = euler(right, direction)
    wave = jnp.maximum(left_wave, right_wave)
    return [
        0.5 * (lf + rf) - 0.5 * wave * (r - l)
        for lf, rf, l, r in zip(left_flux, right_flux, left, right)
    ]


def lane_euler(w, normal):
    inverse = 1.0 / w[0]
    momentum = jnp.where(normal[0], w[1], jnp.where(normal[1], w[2], w[3]))
    speed = momentum * inverse
    pressure = pressure_of(w, inverse)
    flux = [momentum] + [
        w[1 + d] * speed + jnp.where(normal[d], pressure - 1.0, 0.0) for d in range(3)
    ]
    flux.append((w[4] + pressure) * speed)
    return flux, jnp.abs(speed) + jnp.sqrt(1.4 * pressure * inverse)


def load_state(state_ref, points):
    for v in range(5):
        points[v, 0:120, :] = state_ref[v, 0:120, :]
        points[v, 120:125, :] = state_ref[v, 120:125, :]
        points[v, 125:128, :] = state_ref[v, 122:125, :]


def donor_values(points, cell_ref, weight_ref, pair_weight, weight, donor_ref):
    slots = cell_ref.shape[-1]
    grids = donor_ref.shape[0]
    width = slots // grids
    weight[120:128, :] = jnp.zeros((8, slots), jnp.float32)
    for b in range(5):
        for c in range(5):
            row = 5 * b + c
            pair_weight[row : row + 1, :] = weight_ref[1, b] * weight_ref[2, c]
    for a in range(5):
        weight[25 * a : 25 * a + 25, :] = weight_ref[0, a] * pair_weight[0:25, :]
    for tile in range(slots // LANES):
        lanes = slice(tile * LANES, (tile + 1) * LANES)
        index = spread(cell_ref[0:1, lanes], LANES)
        scale = weight[:, lanes]
        first = tile * (LANES // width)
        for v in range(5):
            picked = lane_take(points[v], index)
            donor_ref[first, v : v + 1, :] = jnp.sum(picked * scale, axis=0, keepdims=True)
        for k in range(1, LANES // width):
            donor_ref[first + k, :, :] = pltpu.roll(donor_ref[first], LANES - k * width, axis=1)


def face_slots(points, plus_ref, minus_ref, face_matrix, slot_ref):
    for v in range(5):
        centre = (1.0, 0.0, 0.0, 0.0, 2.5)[v]
        faces = matmul(face_matrix, points[v] - centre) + centre
        for side, order in ((0, plus_ref), (1, minus_ref)):
            for d in range(3):
                start = (side * 3 + d) * ROWS
                slot_ref[side, d, v] = lane_take(
                    faces[start : start + ROWS], spread(order[d : d + 1, :], ROWS)
                )


def face_messages(slot_ref, message_ref):
    count = message_ref.shape[0]
    for row in range(8):
        columns = [
            slot_ref[n // 15, n // 5 % 3, n % 5] for n in range(4 * row, min(4 * row + 4, 30))
        ]
        columns += [columns[-1]] * (4 - len(columns))
        message_ref[:, row, :] = jnp.concatenate(columns, axis=0).T[0:count]


def volume_terms(points, scale_ref, volume_ref, flux, total):
    w = [points[v] for v in range(5)]
    for d in range(3):
        pieces = euler(w, d)[0]
        for v in range(5):
            flux[v, d * LANES : (d + 1) * LANES, :] = pieces[v] * spread(scale_ref[d : d + 1, :], LANES)
    for v in range(5):
        total[v] = matmul(volume_ref[...], flux[v])


def inverse_orders(plus_ref, minus_ref, inverse):
    element = lax.broadcasted_iota(jnp.int32, (LANES, LANES), 0)
    count = lax.broadcasted_iota(jnp.int32, (8, LANES), 1).astype(jnp.float32).astype(jnp.bfloat16)
    for side, order in ((0, plus_ref), (1, minus_ref)):
        for d in range(3):
            chosen = element == spread(order[d : d + 1, :], LANES)
            chosen = jnp.where(chosen, 1.0, 0.0).astype(jnp.bfloat16)
            inverse[side * 3 + d] = lax.dot_general(
                count, chosen, (((1,), (1,)), ((), ())), preferred_element_type=jnp.float32
            ).astype(jnp.int32)


def fringe_picks(pick_ref, pick_rows, pick):
    pick_rows[...] = jnp.zeros(pick_rows.shape, jnp.int32)
    pick_rows[0:1, 0 : pick_ref.shape[1]] = pick_ref[...]
    row = lax.broadcasted_iota(jnp.int32, (8, LANES), 0)
    lane = lax.broadcasted_iota(jnp.int32, (8, LANES), 1)
    block, face = lane // 24, lane // 4 - 6 * (lane // 24)
    side, d = face // 3, face - 3 * (face // 3)
    t = jnp.minimum(8 * block + row, 24)
    number = ((2 * d + 1 - side) * 25 + t) * FRP + lane - 4 * (lane // 4)
    tile, place = number // LANES, number - LANES * (number // LANES)
    value = jnp.zeros((8, LANES), jnp.int32)
    for k in range(pick_rows.shape[1] // LANES):
        source = spread(pick_rows[0:1, k * LANES : (k + 1) * LANES], 8)
        value = jnp.where(tile == k, lane_take(source, place), value)
    pick[...] = value


def fringe_own(slot_ref, remote, own):
    lane = lax.broadcasted_iota(jnp.int32, (8, LANES), 1)
    for v in range(5):
        value = slot_ref[0, 0, v, 0:8, :]
        for k in range(6):
            for block in range(4):
                start = 24 * block + 4 * k
                source = slot_ref[k // 3, k % 3, v, 8 * block : 8 * block + 8, :]
                source = pltpu.roll(source, (start - remote) % LANES, axis=1)
                value = jnp.where((lane >= start) & (lane < start + 4), source, value)
        own[v] = value


def inner_jumps(remote, slot_ref, partner, scale_ref, inverse, jump):
    shared = lax.broadcasted_iota(jnp.int32, (ROWS, LANES), 1) < remote
    for d in range(3):
        high = [slot_ref[0, d, v] for v in range(5)]
        low = [slot_ref[1, d, v] for v in range(5)]

        def other(side, own):
            starts = [((side * 3 + d) * 5 + v) * ROWS for v in range(5)]
            return [jnp.where(shared, partner[s : s + ROWS, :], o) for s, o in zip(starts, own)]

        scale = spread(scale_ref[d : d + 1, :], ROWS)
        for side, value in (
            (0, common(high, other(1, low), d)),
            (1, common(other(0, high), low, d)),
        ):
            back = jnp.concatenate([inverse[side * 3 + d]] * 4, axis=0)
            start = (side * 3 + d) * ROWS
            for v in range(5):
                jump[v, start : start + ROWS, :] = lane_take(value[v], back) * scale


def fringe_jumps(remote, arrived_ref, pick, own, by_grid, scale_ref, inverse, jump):
    parts, slots, width = arrived_ref.shape
    grids = by_grid.shape[0]
    each = parts * slots
    turned = arrived_ref[...].reshape(each, width)
    turned = jnp.concatenate([turned] * (LANES // each), axis=0).T
    by_grid[...] = turned[0 : grids * 8].reshape(grids, 8, LANES)
    chosen = pick[...]
    owner, place = chosen // each, chosen - each * (chosen // each)
    outside = []
    for v in range(5):
        value = lane_take(spread(by_grid[0, v : v + 1, :], 8), place)
        for g in range(1, grids):
            source = lane_take(spread(by_grid[g, v : v + 1, :], 8), place)
            value = jnp.where(owner == g, source, value)
        outside.append(value)
    inside = [own[v] for v in range(5)]
    lane = lax.broadcasted_iota(jnp.int32, (8, LANES), 1)
    face = lane // 4 - 6 * (lane // 24)
    d = face - 3 * (face // 3)
    normal = [d == n for n in range(3)]
    sign = jnp.where(face < 3, 0.5, -0.5)
    outer_flux, outer_wave = lane_euler(outside, normal)
    inner_flux, inner_wave = lane_euler(inside, normal)
    wave = sign * jnp.maximum(outer_wave, inner_wave)
    value = [
        0.5 * (a + b) - wave * (o - i)
        for a, b, o, i in zip(outer_flux, inner_flux, outside, inside)
    ]
    for k in range(6):
        slot = inverse[k] - remote
        here = (slot >= 0) & (slot < FRP)
        slot = jnp.where(here, slot, 0) + 4 * k
        scale = spread(scale_ref[k % 3 : k % 3 + 1, :], 8)
        for block in range(4):
            rows = slice(k * ROWS + 8 * block, k * ROWS + 8 * block + 8)
            for v in range(5):
                new = lane_take(value[v], slot + 24 * block) * scale
                jump[v, rows, :] = jnp.where(here, new, jump[v, rows, :])


def ring_distance(offset, size):
    return min(offset, size - offset)


def kernel(grids, parts, *refs):
    inputs, (out_ref,), buffers, scratch = refs[:10], refs[10:11], refs[11:21], refs[21:]
    (state_ref, scale_ref, plus_ref, minus_ref, cell_ref, weight_ref, pick_ref) = buffers[:7]
    face_ref, volume_ref, lift_ref = buffers[7:]
    (
        points, pair_weight, weight, donor, slot, message, partner_in, gathered, relay, arrived,
        flux, total, inverse, pick_rows, pick, own, partner, jump, by_grid,
        load_sem, sends, recvs,
    ) = scratch
    grid = lax.axis_index("grid")
    part = lax.axis_index("dom")
    across = 4 if parts % 4 == 0 else 1
    down = parts // across

    def part_at(offset):
        z, x = offset // across, offset % across
        return lax.rem(part // across + z, down) * across + lax.rem(lax.rem(part, across) + x, across)

    grid_steps = sorted(range(1, grids), key=lambda k: -ring_distance(k, grids))
    part_steps = sorted(
        range(1, parts),
        key=lambda k: -(ring_distance(k // across, down) + ring_distance(k % across, across)),
    )
    barrier = pltpu.get_barrier_semaphore()
    for k in part_steps:
        pl.semaphore_signal(barrier, inc=1, device_id=(grid, part_at(k)), device_id_type=MESH)
    for k in grid_steps:
        pl.semaphore_signal(
            barrier, inc=1, device_id=(lax.rem(grid + k, grids), part), device_id_type=MESH
        )
    loads = [
        pltpu.make_async_copy(source, target, load_sem.at[n])
        for n, (source, target) in enumerate(zip(inputs, buffers))
    ]
    for n in (0, 4, 5, 2, 3, 7, 1, 6, 8, 9):
        loads[n].start()

    def to_grid(k):
        peer = lax.rem(grid + k, grids)
        return pltpu.make_async_remote_copy(
            src_ref=donor.at[peer], dst_ref=gathered.at[grid],
            send_sem=sends.at[k - 1], recv_sem=recvs.at[k - 1],
            device_id=(peer, part), device_id_type=MESH,
        )

    def to_part(k, source, target, base):
        peer = part_at(k)
        return pltpu.make_async_remote_copy(
            src_ref=source.at[peer], dst_ref=target.at[part],
            send_sem=sends.at[base + k - 1], recv_sem=recvs.at[base + k - 1],
            device_id=(grid, peer), device_id_type=MESH,
        )

    first = [to_grid(k) for k in grid_steps]
    faces = [to_part(k, message, partner_in, grids - 1) for k in part_steps]
    second = [to_part(k, relay, arrived, grids + parts - 2) for k in part_steps]

    loads[0].wait()
    load_state(state_ref, points)
    loads[4].wait()
    loads[5].wait()
    donor_values(points, cell_ref, weight_ref, pair_weight, weight, donor)
    for n in (2, 3, 7):
        loads[n].wait()
    face_slots(points, plus_ref, minus_ref, face_ref[...], slot)
    face_messages(slot, message)

    pl.semaphore_wait(barrier, grids + parts - 2)
    for copy in first:
        copy.start()
    for copy in faces:
        copy.start()
    gathered[grid] = donor[grid]
    partner_in[part] = message[part]

    for n in (1, 6, 8, 9):
        loads[n].wait()
    volume_terms(points, scale_ref, volume_ref, flux, total)
    inverse_orders(plus_ref, minus_ref, inverse)
    fringe_picks(pick_ref, pick_rows, pick)
    fringe_own(slot, parts, own)

    for copy in first:
        copy.wait_recv()
    turned = gathered[...].reshape(grids * 8, LANES)
    if grids * 8 < LANES:
        turned = jnp.concatenate([turned] * (LANES // (grids * 8)), axis=0)
    relay[...] = turned.T[0 : relay.shape[0] * relay.shape[1]].reshape(relay.shape)
    for copy in second:
        copy.start()
    arrived[part] = relay[part]

    for copy in faces:
        copy.wait_recv()
    for row in range(8):
        block = partner_in[:, row, :]
        block = jnp.concatenate([block] * (LANES // parts), axis=0).T
        partner[row * LANES : (row + 1) * LANES, :] = block
    inner_jumps(parts, slot, partner, scale_ref, inverse, jump)

    for copy in second:
        copy.wait_recv()
    fringe_jumps(parts, arrived, pick, own, by_grid, scale_ref, inverse, jump)
    for v in range(5):
        value = total[v] + matmul(lift_ref[...], jump[v])
        out_ref[v] = value[0:125]
    for copy in first + faces + second:
        copy.wait_send()


def body(grids, parts, state, scales, plus, minus, cell, weights, picks):
    f32, i32 = jnp.float32, jnp.int32
    total_slots = cell.shape[-1]
    slots = total_slots // (grids * parts)
    weights = jnp.transpose(weights, (1, 2, 0, 3))
    inputs = (state, scales, plus, minus, cell, weights, picks) + matrices()
    copies = grids - 1 + 2 * (parts - 1)
    pick_tiles = -(-picks.shape[-1] // LANES)
    return pl.pallas_call(
        functools.partial(kernel, grids, parts),
        out_shape=jax.ShapeDtypeStruct(state.shape, f32),
        in_specs=[pl.BlockSpec(memory_space=pl.ANY)] * len(inputs),
        out_specs=pl.BlockSpec(memory_space=pltpu.VMEM),
        scratch_shapes=[pltpu.VMEM(x.shape, x.dtype) for x in inputs]
        + [
            pltpu.VMEM((5, LANES, LANES), f32),
            pltpu.VMEM((32, total_slots), f32),
            pltpu.VMEM((LANES, total_slots), f32),
            pltpu.VMEM((grids, 8, LANES), f32),
            pltpu.VMEM((2, 3, 5, ROWS, LANES), f32),
            pltpu.VMEM((parts, 8, LANES), f32),
            pltpu.VMEM((parts, 8, LANES), f32),
            pltpu.VMEM((grids, 8, LANES), f32),
            pltpu.VMEM((parts, slots, LANES), f32),
            pltpu.VMEM((parts, slots, LANES), f32),
            pltpu.VMEM((5, 3 * LANES, LANES), f32),
            pltpu.VMEM((5, LANES, LANES), f32),
            pltpu.VMEM((6, 8, LANES), i32),
            pltpu.VMEM((8, pick_tiles * LANES), i32),
            pltpu.VMEM((8, LANES), i32),
            pltpu.VMEM((5, 8, LANES), f32),
            pltpu.VMEM((8 * LANES, LANES), f32),
            pltpu.VMEM((5, 6 * ROWS, LANES), f32),
            pltpu.VMEM((grids, 8, LANES), f32),
            pltpu.SemaphoreType.DMA((len(inputs),)),
            pltpu.SemaphoreType.DMA((copies,)),
            pltpu.SemaphoreType.DMA((copies,)),
        ],
        compiler_params=pltpu.CompilerParams(collective_id=0, has_side_effects=True),
        name="step",
    )(*inputs)


def solution(mesh):
    both = ("grid", "dom")
    return jax.shard_map(
        functools.partial(body, mesh.shape["grid"], mesh.shape["dom"]),
        mesh=mesh,
        in_specs=(
            P(None, None, both),
            P(None, both),
            P(None, both),
            P(None, both),
            P(both, None),
            P(both, None, None, None),
            P(both, None),
        ),
        out_specs=P(None, None, both),
        check_vma=False,
    )
```

```python
import functools
import math

import jax
import jax.numpy as jnp
import numpy as np
from jax import lax
from jax.experimental import pallas as pl
from jax.experimental.pallas import tpu as pltpu
from jax.sharding import PartitionSpec as P

MESH = pl.DeviceIdType.MESH
LANES = 128
ROWS = 32
FRP = 4


def gauss_nodes():
    outer = math.sqrt(5.0 + 2.0 * math.sqrt(10.0 / 7.0)) / 3.0
    inner = math.sqrt(5.0 - 2.0 * math.sqrt(10.0 / 7.0)) / 3.0
    return [-outer, -inner, 0.0, inner, outer]


def basis_value(nodes, column, x):
    value = 1.0
    for other in range(5):
        if other != column:
            value = value * (x - nodes[other]) / (nodes[column] - nodes[other])
    return value


def basis_slope(nodes, column, x):
    total = 0.0
    for skipped in range(5):
        if skipped != column:
            value = 1.0 / (nodes[column] - nodes[skipped])
            for other in range(5):
                if other != column and other != skipped:
                    value = value * (x - nodes[other]) / (nodes[column] - nodes[other])
            total = total + value
    return total


def legendre_slopes(x):
    values = [1.0, x]
    slopes = [0.0, 1.0]
    for order in range(1, 5):
        values.append(((2 * order + 1) * x * values[order] - order * values[order - 1]) / (order + 1))
        slopes.append(slopes[order - 1] + (2 * order + 1) * values[order])
    return slopes[4], slopes[5]


def split_point(p, direction):
    index = [p // 25, p // 5 % 5, p % 5]
    along = index.pop(direction)
    return along, 5 * index[0] + index[1]


def split_constant(matrix):
    high = matrix.astype(jnp.bfloat16)
    low = (matrix - high.astype(np.float32)).astype(jnp.bfloat16)
    return jnp.asarray(np.concatenate([high, high, low], axis=1))


def matrices():
    nodes = gauss_nodes()
    deriv = np.array([[basis_slope(nodes, m, x) for m in range(5)] for x in nodes])
    lower = np.array([basis_value(nodes, m, -1.0) for m in range(5)])
    upper = np.array([basis_value(nodes, m, 1.0) for m in range(5)])
    slopes = [legendre_slopes(x) for x in nodes]
    lift_low = np.array([-0.5 * (five - four) for four, five in slopes])
    lift_high = np.array([0.5 * (five + four) for four, five in slopes])
    folded = deriv - np.outer(lift_low, lower) - np.outer(lift_high, upper)
    faces = np.zeros((2, 3, ROWS, LANES))
    volume = np.zeros((LANES, 3, LANES))
    lift = np.zeros((LANES, 2, 3, ROWS))
    for direction in range(3):
        for p in range(125):
            i, t = split_point(p, direction)
            faces[0, direction, t, p] = upper[i]
            faces[1, direction, t, p] = lower[i]
            lift[p, 0, direction, t] = -lift_high[i]
            lift[p, 1, direction, t] = -lift_low[i]
            for other in range(125):
                m, s = split_point(other, direction)
                if s == t:
                    volume[p, direction, other] = -folded[i, m]
    faces[:, :, 25:] = faces[:, :, :1]
    return tuple(
        split_constant(m.astype(np.float32))
        for m in (
            faces.reshape(6 * ROWS, LANES),
            volume.reshape(LANES, 3 * LANES),
            lift.reshape(LANES, 6 * ROWS),
        )
    )


def lane_take(x, index):
    return jnp.take_along_axis(x, index, axis=1, mode="promise_in_bounds")


def spread(row, rows):
    return jnp.broadcast_to(row, (rows, row.shape[-1]))


def store_parts(ref, start, v, value):
    third = ref.shape[0] // 3
    rows, lanes = value.shape[0], slice(v * LANES, (v + 1) * LANES)
    high = value.astype(jnp.bfloat16)
    ref[start : start + rows, lanes] = high
    ref[third + start : third + start + rows, lanes] = (value - high.astype(jnp.float32)).astype(jnp.bfloat16)
    ref[2 * third + start : 2 * third + start + rows, lanes] = high


def products(constant_ref, ref):
    for v in range(0, 5, 2):
        width = min(2, 5 - v) * LANES
        block = jnp.dot(
            constant_ref[...], ref[:, v * LANES : v * LANES + width], preferred_element_type=jnp.float32
        )
        for k in range(width // LANES):
            yield v + k, block[:, k * LANES : (k + 1) * LANES]


def pressure_of(w, inverse):
    square = w[1] * w[1] + w[2] * w[2] + w[3] * w[3]
    return 0.4 * (w[4] - 0.5 * square * inverse)


def euler(w, direction):
    inverse = 1.0 / w[0]
    speed = w[1 + direction] * inverse
    pressure = pressure_of(w, inverse)
    flux = [w[1 + direction]] + [m * speed for m in w[1:4]] + [(w[4] + pressure) * speed]
    flux[1 + direction] = flux[1 + direction] + (pressure - 1.0)
    return flux, jnp.abs(speed) + jnp.sqrt(1.4 * pressure * inverse)


def common(left, right, direction):
    left_flux, left_wave = euler(left, direction)
    right_flux, right_wave = euler(right, direction)
    wave = jnp.maximum(left_wave, right_wave)
    return [
        0.5 * (lf + rf) - 0.5 * wave * (r - l)
        for lf, rf, l, r in zip(left_flux, right_flux, left, right)
    ]


def lane_euler(w, normal):
    inverse = 1.0 / w[0]
    momentum = jnp.where(normal[0], w[1], jnp.where(normal[1], w[2], w[3]))
    speed = momentum * inverse
    pressure = pressure_of(w, inverse)
    flux = [momentum] + [
        w[1 + d] * speed + jnp.where(normal[d], pressure - 1.0, 0.0) for d in range(3)
    ]
    flux.append((w[4] + pressure) * speed)
    return flux, jnp.abs(speed) + jnp.sqrt(1.4 * pressure * inverse)


def load_state(state_ref, points):
    for v in range(5):
        points[v, 0:120, :] = state_ref[v, 0:120, :]
        points[v, 120:125, :] = state_ref[v, 120:125, :]
        points[v, 125:128, :] = state_ref[v, 122:125, :]


def donor_values(points, cell_ref, weight_ref, pair_weight, weight, donor_ref):
    slots = cell_ref.shape[-1]
    grids = donor_ref.shape[0]
    width = slots // grids
    weight[120:128, :] = jnp.zeros((8, slots), jnp.float32)
    for b in range(5):
        for c in range(5):
            row = 5 * b + c
            pair_weight[row : row + 1, :] = weight_ref[1, b] * weight_ref[2, c]
    for a in range(5):
        weight[25 * a : 25 * a + 25, :] = weight_ref[0, a] * pair_weight[0:25, :]
    row = lax.broadcasted_iota(jnp.int32, (8, LANES), 0)
    for tile in range(slots // LANES):
        lanes = slice(tile * LANES, (tile + 1) * LANES)
        index = spread(cell_ref[0:1, lanes], 8)
        sums = [None] * 5
        for k in range(LANES // 8):
            scale = weight[8 * k : 8 * k + 8, lanes]
            for v in range(5):
                term = lane_take(points[v, 8 * k : 8 * k + 8, :], index) * scale
                sums[v] = term if k == 0 else sums[v] + term
        value = jnp.zeros((8, LANES), jnp.float32)
        for v in range(5):
            value = jnp.where(row == v, jnp.sum(sums[v], axis=0, keepdims=True), value)
        first = tile * (LANES // width)
        donor_ref[first] = value
        for k in range(1, LANES // width):
            donor_ref[first + k] = pltpu.roll(value, LANES - k * width, axis=1)


def face_slots(points, plus_ref, minus_ref, face_ref, factor, slot_ref):
    centre = (1.0, 0.0, 0.0, 0.0, 2.5)
    for v in range(5):
        store_parts(factor, 0, v, points[v] - centre[v])
    for v, faces in products(face_ref, factor):
        for side, order in ((0, plus_ref), (1, minus_ref)):
            for d in range(3):
                start = (side * 3 + d) * ROWS
                slot_ref[side, d, v] = centre[v] + lane_take(
                    faces[start : start + ROWS], spread(order[d : d + 1, :], ROWS)
                )


def face_messages(slot_ref, message_ref):
    count = message_ref.shape[0] // 8
    for row in range(8):
        columns = [
            slot_ref[n // 15, n // 5 % 3, n % 5] for n in range(4 * row, min(4 * row + 4, 30))
        ]
        columns += [columns[-1]] * (4 - len(columns))
        message_ref[pl.ds(row, count, stride=8), :] = jnp.concatenate(columns, axis=0).T[0:count]


def partner_faces(partner_in, partner):
    count = partner_in.shape[0] // 8
    for row in range(8):
        block = partner_in[pl.ds(row, count, stride=8), :]
        block = jnp.concatenate([block] * (LANES // count), axis=0).T
        partner[row * LANES : (row + 1) * LANES, :] = block


def volume_terms(points, scale_ref, volume_ref, flux, total):
    w = [points[v] for v in range(5)]
    for d in range(3):
        pieces = euler(w, d)[0]
        for v in range(5):
            store_parts(flux, d * LANES, v, pieces[v] * spread(scale_ref[d : d + 1, :], LANES))
    for v, value in products(volume_ref, flux):
        total[v] = value


def inverse_orders(plus_ref, minus_ref, inverse):
    element = lax.broadcasted_iota(jnp.int32, (LANES, LANES), 0)
    count = lax.broadcasted_iota(jnp.int32, (8, LANES), 1).astype(jnp.float32).astype(jnp.bfloat16)
    for side, order in ((0, plus_ref), (1, minus_ref)):
        for d in range(3):
            chosen = element == spread(order[d : d + 1, :], LANES)
            chosen = jnp.where(chosen, 1.0, 0.0).astype(jnp.bfloat16)
            inverse[side * 3 + d] = lax.dot_general(
                count, chosen, (((1,), (1,)), ((), ())), preferred_element_type=jnp.float32
            ).astype(jnp.int32)


def fringe_picks(pick_ref, pick_rows, pick):
    pick_rows[...] = jnp.zeros(pick_rows.shape, jnp.int32)
    pick_rows[0:1, 0 : pick_ref.shape[1]] = pick_ref[...]
    row = lax.broadcasted_iota(jnp.int32, (8, LANES), 0)
    lane = lax.broadcasted_iota(jnp.int32, (8, LANES), 1)
    block, face = lane // 24, lane // 4 - 6 * (lane // 24)
    side, d = face // 3, face - 3 * (face // 3)
    t = jnp.minimum(8 * block + row, 24)
    number = ((2 * d + 1 - side) * 25 + t) * FRP + lane - 4 * (lane // 4)
    tile, place = number // LANES, number - LANES * (number // LANES)
    value = jnp.zeros((8, LANES), jnp.int32)
    for k in range(pick_rows.shape[1] // LANES):
        source = spread(pick_rows[0:1, k * LANES : (k + 1) * LANES], 8)
        value = jnp.where(tile == k, lane_take(source, place), value)
    pick[...] = value


def fringe_own(slot_ref, remote, own):
    lane = lax.broadcasted_iota(jnp.int32, (8, LANES), 1)
    for v in range(5):
        value = slot_ref[0, 0, v, 0:8, :]
        for k in range(6):
            for block in range(4):
                start = 24 * block + 4 * k
                source = slot_ref[k // 3, k % 3, v, 8 * block : 8 * block + 8, :]
                source = pltpu.roll(source, (start - remote) % LANES, axis=1)
                value = jnp.where((lane >= start) & (lane < start + 4), source, value)
        own[v] = value


def inner_jumps(remote, slot_ref, partner, scale_ref, inverse, jump):
    shared = lax.broadcasted_iota(jnp.int32, (ROWS, LANES), 1) < remote
    for d in range(3):
        high = [slot_ref[0, d, v] for v in range(5)]
        low = [slot_ref[1, d, v] for v in range(5)]

        def other(side, own):
            starts = [((side * 3 + d) * 5 + v) * ROWS for v in range(5)]
            return [jnp.where(shared, partner[s : s + ROWS, :], o) for s, o in zip(starts, own)]

        scale = spread(scale_ref[d : d + 1, :], ROWS)
        for side, value in (
            (0, common(high, other(1, low), d)),
            (1, common(other(0, high), low, d)),
        ):
            back = jnp.concatenate([inverse[side * 3 + d]] * 4, axis=0)
            start = (side * 3 + d) * ROWS
            for v in range(5):
                jump[v, start : start + ROWS, :] = lane_take(value[v], back) * scale


def fringe_jumps(remote, arrived_ref, pick, own, by_grid, scale_ref, inverse, jump, factor):
    parts, slots, width = arrived_ref.shape
    grids = by_grid.shape[0]
    each = parts * slots
    turned = arrived_ref[...].reshape(each, width)
    turned = jnp.concatenate([turned] * (LANES // each), axis=0).T
    by_grid[...] = turned[0 : grids * 8].reshape(grids, 8, LANES)
    chosen = pick[...]
    owner, place = chosen // each, chosen - each * (chosen // each)
    outside = [None] * 5
    for g in range(grids):
        for v in range(5):
            source = lane_take(spread(by_grid[g, v : v + 1, :], 8), place)
            outside[v] = source if g == 0 else jnp.where(owner == g, source, outside[v])
    inside = [own[v] for v in range(5)]
    lane = lax.broadcasted_iota(jnp.int32, (8, LANES), 1)
    face = lane // 4 - 6 * (lane // 24)
    d = face - 3 * (face // 3)
    normal = [d == n for n in range(3)]
    sign = jnp.where(face < 3, 0.5, -0.5)
    outer_flux, outer_wave = lane_euler(outside, normal)
    inner_flux, inner_wave = lane_euler(inside, normal)
    wave = sign * jnp.maximum(outer_wave, inner_wave)
    value = [
        0.5 * (a + b) - wave * (o - i)
        for a, b, o, i in zip(outer_flux, inner_flux, outside, inside)
    ]
    for v in range(5):
        for k in range(6):
            slot = inverse[k] - remote
            here = (slot >= 0) & (slot < FRP)
            slot = jnp.where(here, slot, 0) + 4 * k
            scale = spread(scale_ref[k % 3 : k % 3 + 1, :], 8)
            blocks = []
            for block in range(4):
                start = k * ROWS + 8 * block
                new = lane_take(value[v], slot + 24 * block) * scale
                blocks.append(jnp.where(here, new, jump[v, start : start + 8, :]))
            store_parts(factor, k * ROWS, v, jnp.concatenate(blocks, axis=0))


def ring_distance(offset, size):
    return min(offset, size - offset)


def kernel(grids, parts, *refs):
    inputs, (out_ref,), buffers, scratch = refs[:10], refs[10:11], refs[11:21], refs[21:]
    (state_ref, scale_ref, plus_ref, minus_ref, cell_ref, weight_ref, pick_ref) = buffers[:7]
    face_ref, volume_ref, lift_ref = buffers[7:]
    (
        points, pair_weight, weight, donor, slot, message, partner_in, gathered, relay, arrived,
        face_factor, flux, lift_factor, total, inverse, pick_rows, pick, own, partner, jump, by_grid,
        load_sem, sends, recvs,
    ) = scratch
    loads = [
        pltpu.make_async_copy(source, target, load_sem.at[n])
        for n, (source, target) in enumerate(zip(inputs, buffers))
    ]
    for n in (0, 4, 5):
        loads[n].start()
    grid = lax.axis_index("grid")
    part = lax.axis_index("dom")
    across = 4 if parts % 4 == 0 else 1
    down = parts // across
    z, x = part // across, lax.rem(part, across)
    along_z = [lax.rem(z + k, down) * across for k in range(down)]
    along_x = [lax.rem(x + k, across) for k in range(across)]
    along_grid = [lax.rem(grid + k, grids) for k in range(grids)]

    def part_at(k):
        return along_z[k // across] + along_x[k % across]

    grid_steps = sorted(range(1, grids), key=lambda k: -ring_distance(k, grids))
    part_steps = sorted(
        range(1, parts),
        key=lambda k: -(ring_distance(k // across, down) + ring_distance(k % across, across)),
    )
    barrier = pltpu.get_barrier_semaphore()
    for k in part_steps:
        pl.semaphore_signal(barrier, inc=1, device_id=(grid, part_at(k)), device_id_type=MESH)
    for k in grid_steps:
        pl.semaphore_signal(barrier, inc=1, device_id=(along_grid[k], part), device_id_type=MESH)
    for n in (2, 3, 7, 1, 6, 8, 9):
        loads[n].start()

    def stage(n, source, target, grid_steps=(), part_steps=(), tall=None):
        copies = []
        for k in grid_steps:
            copies.append((along_grid[k], part, along_grid[k], grid))
        for k in part_steps:
            copies.append((grid, part_at(k), part_at(k), part))
        for to_grid, to_part, place, mine in copies:
            if tall is not None:
                place, mine = (pl.ds(pl.multiple_of(p * tall, tall), tall) for p in (place, mine))
            pltpu.make_async_remote_copy(
                src_ref=source.at[place], dst_ref=target.at[mine],
                send_sem=sends.at[n], recv_sem=recvs.at[n],
                device_id=(to_grid, to_part), device_id_type=MESH,
            ).start()

    def finish(semaphore, buffer, count):
        whole = buffer.at[pl.ds(0, count)]
        pltpu.make_async_copy(whole, whole, semaphore).wait()

    loads[0].wait()
    load_state(state_ref, points)
    loads[4].wait()
    loads[5].wait()
    donor_values(points, cell_ref, weight_ref, pair_weight, weight, donor)
    pl.semaphore_wait(barrier, grids + parts - 2)
    stage(0, donor, gathered, grid_steps=grid_steps)
    gathered[grid] = donor[grid]

    for n in (2, 3, 7):
        loads[n].wait()
    face_slots(points, plus_ref, minus_ref, face_ref, face_factor, slot)
    face_messages(slot, message)
    stage(1, message, partner_in, part_steps=part_steps, tall=8)
    mine = pl.ds(pl.multiple_of(part * 8, 8), 8)
    partner_in[mine, :] = message[mine, :]

    for n in (1, 6, 8, 9):
        loads[n].wait()
    volume_terms(points, scale_ref, volume_ref, flux, total)
    inverse_orders(plus_ref, minus_ref, inverse)
    fringe_picks(pick_ref, pick_rows, pick)
    fringe_own(slot, parts, own)

    finish(recvs.at[0], gathered, grids - 1)
    turned = gathered[...].reshape(grids * 8, LANES)
    if grids * 8 < LANES:
        turned = jnp.concatenate([turned] * (LANES // (grids * 8)), axis=0)
    relay[...] = turned.T[0 : relay.shape[0] * relay.shape[1]].reshape(relay.shape)
    stage(2, relay, arrived, part_steps=part_steps)
    arrived[part] = relay[part]

    finish(recvs.at[1], partner_in, 8 * (parts - 1))
    partner_faces(partner_in, partner)
    inner_jumps(parts, slot, partner, scale_ref, inverse, jump)
    finish(sends.at[0], donor, grids - 1)
    finish(sends.at[1], message, 8 * (parts - 1))
    finish(sends.at[2], relay, parts - 1)

    finish(recvs.at[2], arrived, parts - 1)
    fringe_jumps(parts, arrived, pick, own, by_grid, scale_ref, inverse, jump, lift_factor)
    for v, value in products(lift_ref, lift_factor):
        out_ref[v] = (total[v] + value)[0:125]


def body(grids, parts, state, scales, plus, minus, cell, weights, picks):
    f32, i32 = jnp.float32, jnp.int32
    total_slots = cell.shape[-1]
    slots = total_slots // (grids * parts)
    weights = jnp.transpose(weights, (1, 2, 0, 3))
    inputs = (state, scales, plus, minus, cell, weights, picks) + matrices()
    pick_tiles = -(-picks.shape[-1] // LANES)
    return pl.pallas_call(
        functools.partial(kernel, grids, parts),
        out_shape=jax.ShapeDtypeStruct(state.shape, f32),
        in_specs=[pl.BlockSpec(memory_space=pltpu.HBM)] * len(inputs),
        out_specs=pl.BlockSpec(memory_space=pltpu.VMEM),
        scratch_shapes=[pltpu.VMEM(x.shape, x.dtype) for x in inputs]
        + [
            pltpu.VMEM((5, LANES, LANES), f32),
            pltpu.VMEM((32, total_slots), f32),
            pltpu.VMEM((LANES, total_slots), f32),
            pltpu.VMEM((grids, 8, LANES), f32),
            pltpu.VMEM((2, 3, 5, ROWS, LANES), f32),
            pltpu.VMEM((parts * 8, LANES), f32),
            pltpu.VMEM((parts * 8, LANES), f32),
            pltpu.VMEM((grids, 8, LANES), f32),
            pltpu.VMEM((parts, slots, LANES), f32),
            pltpu.VMEM((parts, slots, LANES), f32),
            pltpu.VMEM((3 * LANES, 5 * LANES), jnp.bfloat16),
            pltpu.VMEM((9 * LANES, 5 * LANES), jnp.bfloat16),
            pltpu.VMEM((18 * ROWS, 5 * LANES), jnp.bfloat16),
            pltpu.VMEM((5, LANES, LANES), f32),
            pltpu.VMEM((6, 8, LANES), i32),
            pltpu.VMEM((8, pick_tiles * LANES), i32),
            pltpu.VMEM((8, LANES), i32),
            pltpu.VMEM((5, 8, LANES), f32),
            pltpu.VMEM((8 * LANES, LANES), f32),
            pltpu.VMEM((5, 6 * ROWS, LANES), f32),
            pltpu.VMEM((grids, 8, LANES), f32),
            pltpu.SemaphoreType.DMA((len(inputs),)),
            pltpu.SemaphoreType.DMA((3,)),
            pltpu.SemaphoreType.DMA((3,)),
        ],
        compiler_params=pltpu.CompilerParams(
            collective_id=0, has_side_effects=True, vmem_limit_bytes=24 * 1024 * 1024
        ),
        name="step",
    )(*(pltpu.with_memory_space_constraint(x, pltpu.HBM) for x in inputs))


def solution(mesh):
    both = ("grid", "dom")
    return jax.shard_map(
        functools.partial(body, mesh.shape["grid"], mesh.shape["dom"]),
        mesh=mesh,
        in_specs=(
            P(None, None, both),
            P(None, both),
            P(None, both),
            P(None, both),
            P(both, None),
            P(both, None, None, None),
            P(both, None),
        ),
        out_specs=P(None, None, both),
        check_vma=False,
    )
```

```python
import functools
import math

import jax
import jax.numpy as jnp
import numpy as np
from jax import lax
from jax.experimental import pallas as pl
from jax.experimental.pallas import tpu as pltpu
from jax.sharding import PartitionSpec as P

MESH = pl.DeviceIdType.MESH
LANES = 128
ROWS = 32
FRP = 4


def gauss_nodes():
    outer = math.sqrt(5.0 + 2.0 * math.sqrt(10.0 / 7.0)) / 3.0
    inner = math.sqrt(5.0 - 2.0 * math.sqrt(10.0 / 7.0)) / 3.0
    return [-outer, -inner, 0.0, inner, outer]


def basis_value(nodes, column, x):
    value = 1.0
    for other in range(5):
        if other != column:
            value = value * (x - nodes[other]) / (nodes[column] - nodes[other])
    return value


def basis_slope(nodes, column, x):
    total = 0.0
    for skipped in range(5):
        if skipped != column:
            value = 1.0 / (nodes[column] - nodes[skipped])
            for other in range(5):
                if other != column and other != skipped:
                    value = value * (x - nodes[other]) / (nodes[column] - nodes[other])
            total = total + value
    return total


def legendre_slopes(x):
    values = [1.0, x]
    slopes = [0.0, 1.0]
    for order in range(1, 5):
        values.append(((2 * order + 1) * x * values[order] - order * values[order - 1]) / (order + 1))
        slopes.append(slopes[order - 1] + (2 * order + 1) * values[order])
    return slopes[4], slopes[5]


def split_point(p, direction):
    index = [p // 25, p // 5 % 5, p % 5]
    along = index.pop(direction)
    return along, 5 * index[0] + index[1]


def split_constant(matrix):
    high = matrix.astype(jnp.bfloat16)
    low = (matrix - high.astype(np.float32)).astype(jnp.bfloat16)
    return jnp.asarray(np.concatenate([high, high, low], axis=1))


def matrices():
    nodes = gauss_nodes()
    deriv = np.array([[basis_slope(nodes, m, x) for m in range(5)] for x in nodes])
    lower = np.array([basis_value(nodes, m, -1.0) for m in range(5)])
    upper = np.array([basis_value(nodes, m, 1.0) for m in range(5)])
    slopes = [legendre_slopes(x) for x in nodes]
    lift_low = np.array([-0.5 * (five - four) for four, five in slopes])
    lift_high = np.array([0.5 * (five + four) for four, five in slopes])
    folded = deriv - np.outer(lift_low, lower) - np.outer(lift_high, upper)
    faces = np.zeros((2, 3, ROWS, LANES))
    volume = np.zeros((LANES, 3, LANES))
    lift = np.zeros((LANES, 2, 3, ROWS))
    for direction in range(3):
        for p in range(125):
            i, t = split_point(p, direction)
            faces[0, direction, t, p] = upper[i]
            faces[1, direction, t, p] = lower[i]
            lift[p, 0, direction, t] = -lift_high[i]
            lift[p, 1, direction, t] = -lift_low[i]
            for other in range(125):
                m, s = split_point(other, direction)
                if s == t:
                    volume[p, direction, other] = -folded[i, m]
    faces[:, :, 25:] = faces[:, :, :1]
    return tuple(
        split_constant(m.astype(np.float32))
        for m in (
            faces.reshape(6 * ROWS, LANES),
            volume.reshape(LANES, 3 * LANES),
            lift.reshape(LANES, 6 * ROWS),
        )
    )


def lane_take(x, index):
    return jnp.take_along_axis(x, index, axis=1, mode="promise_in_bounds")


def spread(row, rows):
    return jnp.broadcast_to(row, (rows, row.shape[-1]))


def store_parts(ref, start, v, value):
    third = ref.shape[0] // 3
    rows, lanes = value.shape[0], slice(v * LANES, (v + 1) * LANES)
    high = value.astype(jnp.bfloat16)
    ref[start : start + rows, lanes] = high
    ref[third + start : third + start + rows, lanes] = (value - high.astype(jnp.float32)).astype(jnp.bfloat16)
    ref[2 * third + start : 2 * third + start + rows, lanes] = high


def products(constant_ref, ref):
    for v in range(0, 5, 2):
        width = min(2, 5 - v) * LANES
        block = jnp.dot(
            constant_ref[...], ref[:, v * LANES : v * LANES + width], preferred_element_type=jnp.float32
        )
        for k in range(width // LANES):
            yield v + k, block[:, k * LANES : (k + 1) * LANES]


def pressure_of(w, inverse):
    square = w[1] * w[1] + w[2] * w[2] + w[3] * w[3]
    return 0.4 * (w[4] - 0.5 * square * inverse)


def euler(w, direction):
    inverse = 1.0 / w[0]
    speed = w[1 + direction] * inverse
    pressure = pressure_of(w, inverse)
    flux = [w[1 + direction]] + [m * speed for m in w[1:4]] + [(w[4] + pressure) * speed]
    flux[1 + direction] = flux[1 + direction] + (pressure - 1.0)
    return flux, jnp.abs(speed) + jnp.sqrt(1.4 * pressure * inverse)


def common(left, right, direction):
    left_flux, left_wave = euler(left, direction)
    right_flux, right_wave = euler(right, direction)
    wave = jnp.maximum(left_wave, right_wave)
    return [
        0.5 * (lf + rf) - 0.5 * wave * (r - l)
        for lf, rf, l, r in zip(left_flux, right_flux, left, right)
    ]


def lane_euler(w, normal):
    inverse = 1.0 / w[0]
    momentum = jnp.where(normal[0], w[1], jnp.where(normal[1], w[2], w[3]))
    speed = momentum * inverse
    pressure = pressure_of(w, inverse)
    flux = [momentum] + [
        w[1 + d] * speed + jnp.where(normal[d], pressure - 1.0, 0.0) for d in range(3)
    ]
    flux.append((w[4] + pressure) * speed)
    return flux, jnp.abs(speed) + jnp.sqrt(1.4 * pressure * inverse)


def load_state(state_ref, points):
    for v in range(5):
        points[v, 0:120, :] = state_ref[v, 0:120, :]
        points[v, 120:125, :] = state_ref[v, 120:125, :]
        points[v, 125:128, :] = state_ref[v, 122:125, :]


def donor_tile(tile, points, cell_ref, weight_ref, pair_weight, weight, donor_ref):
    per_tile = LANES * donor_ref.shape[0] // cell_ref.shape[-1]
    lanes = pl.ds(pl.multiple_of(tile * LANES, LANES), LANES)
    scales = [[weight_ref[d, k, :, lanes] for k in range(5)] for d in range(3)]
    for b in range(5):
        for c in range(5):
            row = 5 * b + c
            pair_weight[row : row + 1, :] = scales[1][b] * scales[2][c]
    weight[120:128, :] = jnp.zeros((8, LANES), jnp.float32)
    for a in range(5):
        weight[25 * a : 25 * a + 25, :] = scales[0][a] * pair_weight[0:25, :]
    index = spread(cell_ref[0:1, lanes], 8)
    sums = [None] * 5
    for k in range(LANES // 8):
        scale = weight[8 * k : 8 * k + 8, :]
        for v in range(5):
            term = lane_take(points[v, 8 * k : 8 * k + 8, :], index) * scale
            sums[v] = term if k == 0 else sums[v] + term
    row = lax.broadcasted_iota(jnp.int32, (8, LANES), 0)
    value = jnp.zeros((8, LANES), jnp.float32)
    for v in range(5):
        value = jnp.where(row == v, jnp.sum(sums[v], axis=0, keepdims=True), value)
    donor_ref[tile * per_tile] = value
    for k in range(1, per_tile):
        donor_ref[tile * per_tile + k] = pltpu.roll(value, LANES - k * (LANES // per_tile), axis=1)


def face_slots(points, plus_ref, minus_ref, face_ref, factor, slot_ref):
    centre = (1.0, 0.0, 0.0, 0.0, 2.5)
    for v in range(5):
        store_parts(factor, 0, v, points[v] - centre[v])
    for v, faces in products(face_ref, factor):
        for side, order in ((0, plus_ref), (1, minus_ref)):
            for d in range(3):
                start = (side * 3 + d) * ROWS
                slot_ref[side, d, v] = centre[v] + lane_take(
                    faces[start : start + ROWS], spread(order[d : d + 1, :], ROWS)
                )


def face_messages(slot_ref, message_ref):
    count = message_ref.shape[0] // 8
    for row in range(8):
        columns = [
            slot_ref[n // 15, n // 5 % 3, n % 5] for n in range(4 * row, min(4 * row + 4, 30))
        ]
        columns += [columns[-1]] * (4 - len(columns))
        message_ref[pl.ds(row, count, stride=8), :] = jnp.concatenate(columns, axis=0).T[0:count]


def partner_faces(partner_in, partner):
    count = partner_in.shape[0] // 8
    for row in range(8):
        block = partner_in[pl.ds(row, count, stride=8), :]
        block = jnp.concatenate([block] * (LANES // count), axis=0).T
        partner[row * LANES : (row + 1) * LANES, :] = block


def volume_terms(points, scale_ref, volume_ref, flux, total):
    w = [points[v] for v in range(5)]
    for d in range(3):
        pieces = euler(w, d)[0]
        for v in range(5):
            store_parts(flux, d * LANES, v, pieces[v] * spread(scale_ref[d : d + 1, :], LANES))
    for v, value in products(volume_ref, flux):
        total[v] = value


def inverse_orders(plus_ref, minus_ref, inverse):
    element = lax.broadcasted_iota(jnp.int32, (LANES, LANES), 0)
    count = lax.broadcasted_iota(jnp.int32, (8, LANES), 1).astype(jnp.float32).astype(jnp.bfloat16)
    for side, order in ((0, plus_ref), (1, minus_ref)):
        for d in range(3):
            chosen = element == spread(order[d : d + 1, :], LANES)
            chosen = jnp.where(chosen, 1.0, 0.0).astype(jnp.bfloat16)
            inverse[side * 3 + d] = lax.dot_general(
                count, chosen, (((1,), (1,)), ((), ())), preferred_element_type=jnp.float32
            ).astype(jnp.int32)


def fringe_picks(pick_ref, pick_rows, pick):
    pick_rows[...] = jnp.zeros(pick_rows.shape, jnp.int32)
    pick_rows[0:1, 0 : pick_ref.shape[1]] = pick_ref[...]
    row = lax.broadcasted_iota(jnp.int32, (8, LANES), 0)
    lane = lax.broadcasted_iota(jnp.int32, (8, LANES), 1)
    block, face = lane // 24, lane // 4 - 6 * (lane // 24)
    side, d = face // 3, face - 3 * (face // 3)
    t = jnp.minimum(8 * block + row, 24)
    number = ((2 * d + 1 - side) * 25 + t) * FRP + lane - 4 * (lane // 4)
    tile, place = number // LANES, number - LANES * (number // LANES)
    value = jnp.zeros((8, LANES), jnp.int32)
    for k in range(pick_rows.shape[1] // LANES):
        source = spread(pick_rows[0:1, k * LANES : (k + 1) * LANES], 8)
        value = jnp.where(tile == k, lane_take(source, place), value)
    pick[...] = value


def fringe_own(slot_ref, remote, own):
    lane = lax.broadcasted_iota(jnp.int32, (8, LANES), 1)
    for v in range(5):
        value = slot_ref[0, 0, v, 0:8, :]
        for k in range(6):
            for block in range(4):
                start = 24 * block + 4 * k
                source = slot_ref[k // 3, k % 3, v, 8 * block : 8 * block + 8, :]
                source = pltpu.roll(source, (start - remote) % LANES, axis=1)
                value = jnp.where((lane >= start) & (lane < start + 4), source, value)
        own[v] = value


def inner_jumps(remote, slot_ref, partner, scale_ref, inverse, jump):
    shared = lax.broadcasted_iota(jnp.int32, (ROWS, LANES), 1) < remote
    for d in range(3):
        high = [slot_ref[0, d, v] for v in range(5)]
        low = [slot_ref[1, d, v] for v in range(5)]

        def other(side, own):
            starts = [((side * 3 + d) * 5 + v) * ROWS for v in range(5)]
            return [jnp.where(shared, partner[s : s + ROWS, :], o) for s, o in zip(starts, own)]

        scale = spread(scale_ref[d : d + 1, :], ROWS)
        for side, value in (
            (0, common(high, other(1, low), d)),
            (1, common(other(0, high), low, d)),
        ):
            back = jnp.concatenate([inverse[side * 3 + d]] * 4, axis=0)
            start = (side * 3 + d) * ROWS
            for v in range(5):
                jump[v, start : start + ROWS, :] = lane_take(value[v], back) * scale


def fringe_jumps(remote, arrived_ref, pick, own, by_grid, scale_ref, inverse, jump, factor):
    parts, slots, width = arrived_ref.shape
    grids = by_grid.shape[0]
    each = parts * slots
    turned = arrived_ref[...].reshape(each, width)
    turned = jnp.concatenate([turned] * (LANES // each), axis=0).T
    by_grid[...] = turned[0 : grids * 8].reshape(grids, 8, LANES)
    chosen = pick[...]
    owner, place = chosen // each, chosen - each * (chosen // each)
    outside = [None] * 5
    for g in range(grids):
        for v in range(5):
            source = lane_take(spread(by_grid[g, v : v + 1, :], 8), place)
            outside[v] = source if g == 0 else jnp.where(owner == g, source, outside[v])
    inside = [own[v] for v in range(5)]
    lane = lax.broadcasted_iota(jnp.int32, (8, LANES), 1)
    face = lane // 4 - 6 * (lane // 24)
    d = face - 3 * (face // 3)
    normal = [d == n for n in range(3)]
    sign = jnp.where(face < 3, 0.5, -0.5)
    outer_flux, outer_wave = lane_euler(outside, normal)
    inner_flux, inner_wave = lane_euler(inside, normal)
    wave = sign * jnp.maximum(outer_wave, inner_wave)
    value = [
        0.5 * (a + b) - wave * (o - i)
        for a, b, o, i in zip(outer_flux, inner_flux, outside, inside)
    ]
    for v in range(5):
        for k in range(6):
            slot = inverse[k] - remote
            here = (slot >= 0) & (slot < FRP)
            slot = jnp.where(here, slot, 0) + 4 * k
            scale = spread(scale_ref[k % 3 : k % 3 + 1, :], 8)
            blocks = []
            for block in range(4):
                start = k * ROWS + 8 * block
                new = lane_take(value[v], slot + 24 * block) * scale
                blocks.append(jnp.where(here, new, jump[v, start : start + 8, :]))
            store_parts(factor, k * ROWS, v, jnp.concatenate(blocks, axis=0))


def ring_distance(offset, size):
    return min(offset, size - offset)


def kernel(grids, parts, *refs):
    inputs, (out_ref,), buffers, scratch = refs[:10], refs[10:11], refs[11:21], refs[21:]
    (state_ref, scale_ref, plus_ref, minus_ref, cell_ref, weight_ref, pick_ref) = buffers[:7]
    face_ref, volume_ref, lift_ref = buffers[7:]
    (
        points, pair_weight, weight, donor, slot, message, partner_in, gathered, relay, arrived,
        face_factor, flux, lift_factor, total, inverse, pick_rows, pick, own, partner, jump, by_grid,
        load_sem, sends, recvs,
    ) = scratch
    loads = [
        pltpu.make_async_copy(source, target, load_sem.at[n])
        for n, (source, target) in enumerate(zip(inputs, buffers))
    ]
    for n in (0, 4, 5):
        loads[n].start()
    grid = lax.axis_index("grid")
    part = lax.axis_index("dom")
    across = 4 if parts % 4 == 0 else 1
    down = parts // across
    z, x = part // across, lax.rem(part, across)
    along_z = [lax.rem(z + k, down) * across for k in range(down)]
    along_x = [lax.rem(x + k, across) for k in range(across)]
    along_grid = [lax.rem(grid + k, grids) for k in range(grids)]

    def part_at(k):
        return along_z[k // across] + along_x[k % across]

    grid_steps = sorted(range(1, grids), key=lambda k: -ring_distance(k, grids))
    part_steps = sorted(
        range(1, parts),
        key=lambda k: -(ring_distance(k // across, down) + ring_distance(k % across, across)),
    )
    barrier = pltpu.get_barrier_semaphore()
    for k in part_steps:
        pl.semaphore_signal(barrier, inc=1, device_id=(grid, part_at(k)), device_id_type=MESH)
    for k in grid_steps:
        pl.semaphore_signal(barrier, inc=1, device_id=(along_grid[k], part), device_id_type=MESH)
    for n in (2, 3, 7, 1, 6, 8, 9):
        loads[n].start()

    def send(n, source, place, target, mine, to_grid, to_part):
        pltpu.make_async_remote_copy(
            src_ref=source.at[place], dst_ref=target.at[mine],
            send_sem=sends.at[n], recv_sem=recvs.at[n],
            device_id=(to_grid, to_part), device_id_type=MESH,
        ).start()

    def finish(semaphore, buffer, count):
        whole = buffer.at[pl.ds(0, count)]
        pltpu.make_async_copy(whole, whole, semaphore).wait()

    loads[0].wait()
    load_state(state_ref, points)
    loads[4].wait()
    loads[5].wait()
    tiles = cell_ref.shape[-1] // LANES
    per_tile = grids // tiles
    near = grid // per_tile
    for n, step in enumerate(sorted(range(tiles), key=lambda k: -ring_distance(k, tiles))):
        tile = lax.rem(near + step, tiles)
        donor_tile(
            tile, points, cell_ref, weight_ref, pair_weight.at[n % 2], weight.at[n % 2], donor
        )
        if n == 0:
            pl.semaphore_wait(barrier, grids + parts - 2)
        for k in range(per_tile if step else per_tile - 1):
            first = lax.rem(grid, per_tile) + 1 if step == 0 else 0
            peer = tile * per_tile + lax.rem(first + k, per_tile)
            send(0, donor, peer, gathered, grid, peer, part)
    gathered[grid] = donor[grid]

    for n in (2, 3, 7):
        loads[n].wait()
    face_slots(points, plus_ref, minus_ref, face_ref, face_factor, slot)
    face_messages(slot, message)
    mine = pl.ds(pl.multiple_of(part * 8, 8), 8)
    for k in part_steps:
        peer = part_at(k)
        send(1, message, pl.ds(pl.multiple_of(peer * 8, 8), 8), partner_in, mine, grid, peer)
    partner_in[mine, :] = message[mine, :]

    for n in (1, 6, 8, 9):
        loads[n].wait()
    volume_terms(points, scale_ref, volume_ref, flux, total)
    inverse_orders(plus_ref, minus_ref, inverse)
    fringe_picks(pick_ref, pick_rows, pick)
    fringe_own(slot, parts, own)

    finish(recvs.at[0], gathered, grids - 1)
    turned = gathered[...].reshape(grids * 8, LANES)
    if grids * 8 < LANES:
        turned = jnp.concatenate([turned] * (LANES // (grids * 8)), axis=0)
    relay[...] = turned.T[0 : relay.shape[0] * relay.shape[1]].reshape(relay.shape)
    for k in part_steps:
        peer = part_at(k)
        send(2, relay, peer, arrived, part, grid, peer)
    arrived[part] = relay[part]

    finish(recvs.at[1], partner_in, 8 * (parts - 1))
    partner_faces(partner_in, partner)
    inner_jumps(parts, slot, partner, scale_ref, inverse, jump)
    finish(sends.at[0], donor, grids - 1)
    finish(sends.at[1], message, 8 * (parts - 1))
    finish(sends.at[2], relay, parts - 1)

    finish(recvs.at[2], arrived, parts - 1)
    fringe_jumps(parts, arrived, pick, own, by_grid, scale_ref, inverse, jump, lift_factor)
    for v, value in products(lift_ref, lift_factor):
        out_ref[v] = (total[v] + value)[0:125]


def body(grids, parts, state, scales, plus, minus, cell, weights, picks):
    f32, i32 = jnp.float32, jnp.int32
    total_slots = cell.shape[-1]
    slots = total_slots // (grids * parts)
    weights = jnp.transpose(weights, (1, 2, 0, 3))
    inputs = (state, scales, plus, minus, cell, weights, picks) + matrices()
    pick_tiles = -(-picks.shape[-1] // LANES)
    return pl.pallas_call(
        functools.partial(kernel, grids, parts),
        out_shape=jax.ShapeDtypeStruct(state.shape, f32),
        in_specs=[pl.BlockSpec(memory_space=pltpu.HBM)] * len(inputs),
        out_specs=pl.BlockSpec(memory_space=pltpu.VMEM),
        scratch_shapes=[pltpu.VMEM(x.shape, x.dtype) for x in inputs]
        + [
            pltpu.VMEM((5, LANES, LANES), f32),
            pltpu.VMEM((2, 32, LANES), f32),
            pltpu.VMEM((2, LANES, LANES), f32),
            pltpu.VMEM((grids, 8, LANES), f32),
            pltpu.VMEM((2, 3, 5, ROWS, LANES), f32),
            pltpu.VMEM((parts * 8, LANES), f32),
            pltpu.VMEM((parts * 8, LANES), f32),
            pltpu.VMEM((grids, 8, LANES), f32),
            pltpu.VMEM((parts, slots, LANES), f32),
            pltpu.VMEM((parts, slots, LANES), f32),
            pltpu.VMEM((3 * LANES, 5 * LANES), jnp.bfloat16),
            pltpu.VMEM((9 * LANES, 5 * LANES), jnp.bfloat16),
            pltpu.VMEM((18 * ROWS, 5 * LANES), jnp.bfloat16),
            pltpu.VMEM((5, LANES, LANES), f32),
            pltpu.VMEM((6, 8, LANES), i32),
            pltpu.VMEM((8, pick_tiles * LANES), i32),
            pltpu.VMEM((8, LANES), i32),
            pltpu.VMEM((5, 8, LANES), f32),
            pltpu.VMEM((8 * LANES, LANES), f32),
            pltpu.VMEM((5, 6 * ROWS, LANES), f32),
            pltpu.VMEM((grids, 8, LANES), f32),
            pltpu.SemaphoreType.DMA((len(inputs),)),
            pltpu.SemaphoreType.DMA((3,)),
            pltpu.SemaphoreType.DMA((3,)),
        ],
        compiler_params=pltpu.CompilerParams(
            collective_id=0, has_side_effects=True, vmem_limit_bytes=24 * 1024 * 1024
        ),
        name="step",
    )(*(pltpu.with_memory_space_constraint(x, pltpu.HBM) for x in inputs))


def solution(mesh):
    both = ("grid", "dom")
    return jax.shard_map(
        functools.partial(body, mesh.shape["grid"], mesh.shape["dom"]),
        mesh=mesh,
        in_specs=(
            P(None, None, both),
            P(None, both),
            P(None, both),
            P(None, both),
            P(both, None),
            P(both, None, None, None),
            P(both, None),
        ),
        out_specs=P(None, None, both),
        check_vma=False,
    )
```

```python
import functools
import math

import jax
import jax.numpy as jnp
import numpy as np
from jax import lax
from jax.experimental import pallas as pl
from jax.experimental.pallas import tpu as pltpu
from jax.sharding import PartitionSpec as P

MESH = pl.DeviceIdType.MESH
LANES = 128
ROWS = 32
FRP = 4


def gauss_nodes():
    outer = math.sqrt(5.0 + 2.0 * math.sqrt(10.0 / 7.0)) / 3.0
    inner = math.sqrt(5.0 - 2.0 * math.sqrt(10.0 / 7.0)) / 3.0
    return [-outer, -inner, 0.0, inner, outer]


def basis_value(nodes, column, x):
    value = 1.0
    for other in range(5):
        if other != column:
            value = value * (x - nodes[other]) / (nodes[column] - nodes[other])
    return value


def basis_slope(nodes, column, x):
    total = 0.0
    for skipped in range(5):
        if skipped != column:
            value = 1.0 / (nodes[column] - nodes[skipped])
            for other in range(5):
                if other != column and other != skipped:
                    value = value * (x - nodes[other]) / (nodes[column] - nodes[other])
            total = total + value
    return total


def legendre_slopes(x):
    values = [1.0, x]
    slopes = [0.0, 1.0]
    for order in range(1, 5):
        values.append(((2 * order + 1) * x * values[order] - order * values[order - 1]) / (order + 1))
        slopes.append(slopes[order - 1] + (2 * order + 1) * values[order])
    return slopes[4], slopes[5]


def split_point(p, direction):
    index = [p // 25, p // 5 % 5, p % 5]
    along = index.pop(direction)
    return along, 5 * index[0] + index[1]


def split_constant(matrix):
    high = matrix.astype(jnp.bfloat16)
    low = (matrix - high.astype(np.float32)).astype(jnp.bfloat16)
    return jnp.asarray(np.concatenate([high, high, low], axis=1))


def matrices():
    nodes = gauss_nodes()
    deriv = np.array([[basis_slope(nodes, m, x) for m in range(5)] for x in nodes])
    lower = np.array([basis_value(nodes, m, -1.0) for m in range(5)])
    upper = np.array([basis_value(nodes, m, 1.0) for m in range(5)])
    slopes = [legendre_slopes(x) for x in nodes]
    lift_low = np.array([-0.5 * (five - four) for four, five in slopes])
    lift_high = np.array([0.5 * (five + four) for four, five in slopes])
    folded = deriv - np.outer(lift_low, lower) - np.outer(lift_high, upper)
    faces = np.zeros((2, 3, ROWS, LANES))
    volume = np.zeros((LANES, 3, LANES))
    lift = np.zeros((LANES, 2, 3, ROWS))
    for direction in range(3):
        for p in range(125):
            i, t = split_point(p, direction)
            faces[0, direction, t, p] = upper[i]
            faces[1, direction, t, p] = lower[i]
            lift[p, 0, direction, t] = -lift_high[i]
            lift[p, 1, direction, t] = -lift_low[i]
            for other in range(125):
                m, s = split_point(other, direction)
                if s == t:
                    volume[p, direction, other] = -folded[i, m]
    faces[:, :, 25:] = faces[:, :, :1]
    return tuple(
        split_constant(m.astype(np.float32))
        for m in (
            faces.reshape(6 * ROWS, LANES),
            volume.reshape(LANES, 3 * LANES),
            lift.reshape(LANES, 6 * ROWS),
        )
    )


def lane_take(x, index):
    return jnp.take_along_axis(x, index, axis=1, mode="promise_in_bounds")


def spread(row, rows):
    return jnp.broadcast_to(row, (rows, row.shape[-1]))


def store_parts(ref, start, v, value):
    third = ref.shape[0] // 3
    rows, lanes = value.shape[0], slice(v * LANES, (v + 1) * LANES)
    high = value.astype(jnp.bfloat16)
    ref[start : start + rows, lanes] = high
    ref[third + start : third + start + rows, lanes] = (value - high.astype(jnp.float32)).astype(jnp.bfloat16)
    ref[2 * third + start : 2 * third + start + rows, lanes] = high


def products(constant_ref, ref):
    for v in range(0, 5, 2):
        width = min(2, 5 - v) * LANES
        block = jnp.dot(
            constant_ref[...], ref[:, v * LANES : v * LANES + width], preferred_element_type=jnp.float32
        )
        for k in range(width // LANES):
            yield v + k, block[:, k * LANES : (k + 1) * LANES]


def pressure_of(w, inverse):
    square = w[1] * w[1] + w[2] * w[2] + w[3] * w[3]
    return 0.4 * (w[4] - 0.5 * square * inverse)


def euler(w, direction):
    inverse = 1.0 / w[0]
    speed = w[1 + direction] * inverse
    pressure = pressure_of(w, inverse)
    flux = [w[1 + direction]] + [m * speed for m in w[1:4]] + [(w[4] + pressure) * speed]
    flux[1 + direction] = flux[1 + direction] + (pressure - 1.0)
    return flux, jnp.abs(speed) + jnp.sqrt(1.4 * pressure * inverse)


def common(left, right, direction):
    left_flux, left_wave = euler(left, direction)
    right_flux, right_wave = euler(right, direction)
    wave = jnp.maximum(left_wave, right_wave)
    return [
        0.5 * (lf + rf) - 0.5 * wave * (r - l)
        for lf, rf, l, r in zip(left_flux, right_flux, left, right)
    ]


def lane_euler(w, normal):
    inverse = 1.0 / w[0]
    momentum = jnp.where(normal[0], w[1], jnp.where(normal[1], w[2], w[3]))
    speed = momentum * inverse
    pressure = pressure_of(w, inverse)
    flux = [momentum] + [
        w[1 + d] * speed + jnp.where(normal[d], pressure - 1.0, 0.0) for d in range(3)
    ]
    flux.append((w[4] + pressure) * speed)
    return flux, jnp.abs(speed) + jnp.sqrt(1.4 * pressure * inverse)


def load_state(state_ref, points):
    for v in range(5):
        points[v, 0:120, :] = state_ref[v, 0:120, :]
        points[v, 120:125, :] = state_ref[v, 120:125, :]
        points[v, 125:128, :] = state_ref[v, 122:125, :]


def donor_tile(tile, points, cell_ref, weight_ref, pair_weight, weight, donor_ref):
    per_tile = LANES * donor_ref.shape[0] // cell_ref.shape[-1]
    lanes = slice(tile * LANES, (tile + 1) * LANES)
    scales = [[weight_ref[d, k, :, lanes] for k in range(5)] for d in range(3)]
    for b in range(5):
        for c in range(5):
            row = 5 * b + c
            pair_weight[row : row + 1, :] = scales[1][b] * scales[2][c]
    weight[120:128, :] = jnp.zeros((8, LANES), jnp.float32)
    for a in range(5):
        weight[25 * a : 25 * a + 25, :] = scales[0][a] * pair_weight[0:25, :]
    index = spread(cell_ref[0:1, lanes], 8)
    sums = [None] * 5
    for k in range(LANES // 8):
        scale = weight[8 * k : 8 * k + 8, :]
        for v in range(5):
            term = lane_take(points[v, 8 * k : 8 * k + 8, :], index) * scale
            sums[v] = term if k == 0 else sums[v] + term
    row = lax.broadcasted_iota(jnp.int32, (8, LANES), 0)
    value = jnp.zeros((8, LANES), jnp.float32)
    for v in range(5):
        value = jnp.where(row == v, jnp.sum(sums[v], axis=0, keepdims=True), value)
    donor_ref[tile * per_tile] = value
    for k in range(1, per_tile):
        donor_ref[tile * per_tile + k] = pltpu.roll(value, LANES - k * (LANES // per_tile), axis=1)


def face_slots(points, plus_ref, minus_ref, face_ref, factor, slot_ref):
    centre = (1.0, 0.0, 0.0, 0.0, 2.5)
    for v in range(5):
        store_parts(factor, 0, v, points[v] - centre[v])
    for v, faces in products(face_ref, factor):
        for side, order in ((0, plus_ref), (1, minus_ref)):
            for d in range(3):
                start = (side * 3 + d) * ROWS
                slot_ref[side, d, v] = centre[v] + lane_take(
                    faces[start : start + ROWS], spread(order[d : d + 1, :], ROWS)
                )


def face_messages(slot_ref, message_ref):
    count = message_ref.shape[0] // 8
    for row in range(8):
        columns = [
            slot_ref[n // 15, n // 5 % 3, n % 5] for n in range(4 * row, min(4 * row + 4, 30))
        ]
        columns += [columns[-1]] * (4 - len(columns))
        message_ref[pl.ds(row, count, stride=8), :] = jnp.concatenate(columns, axis=0).T[0:count]


def partner_faces(partner_in, partner):
    count = partner_in.shape[0] // 8
    for row in range(8):
        block = partner_in[pl.ds(row, count, stride=8), :]
        block = jnp.concatenate([block] * (LANES // count), axis=0).T
        partner[row * LANES : (row + 1) * LANES, :] = block


def volume_terms(points, scale_ref, volume_ref, flux, total):
    w = [points[v] for v in range(5)]
    for d in range(3):
        pieces = euler(w, d)[0]
        for v in range(5):
            store_parts(flux, d * LANES, v, pieces[v] * spread(scale_ref[d : d + 1, :], LANES))
    for v, value in products(volume_ref, flux):
        total[v] = value


def inverse_orders(plus_ref, minus_ref, inverse):
    element = lax.broadcasted_iota(jnp.int32, (LANES, LANES), 0)
    count = lax.broadcasted_iota(jnp.int32, (8, LANES), 1).astype(jnp.float32).astype(jnp.bfloat16)
    for side, order in ((0, plus_ref), (1, minus_ref)):
        for d in range(3):
            chosen = element == spread(order[d : d + 1, :], LANES)
            chosen = jnp.where(chosen, 1.0, 0.0).astype(jnp.bfloat16)
            inverse[side * 3 + d] = lax.dot_general(
                count, chosen, (((1,), (1,)), ((), ())), preferred_element_type=jnp.float32
            ).astype(jnp.int32)


def fringe_picks(pick_ref, pick_rows, pick):
    pick_rows[...] = jnp.zeros(pick_rows.shape, jnp.int32)
    pick_rows[0:1, 0 : pick_ref.shape[1]] = pick_ref[...]
    row = lax.broadcasted_iota(jnp.int32, (8, LANES), 0)
    lane = lax.broadcasted_iota(jnp.int32, (8, LANES), 1)
    block, face = lane // 24, lane // 4 - 6 * (lane // 24)
    side, d = face // 3, face - 3 * (face // 3)
    t = jnp.minimum(8 * block + row, 24)
    number = ((2 * d + 1 - side) * 25 + t) * FRP + lane - 4 * (lane // 4)
    tile, place = number // LANES, number - LANES * (number // LANES)
    value = jnp.zeros((8, LANES), jnp.int32)
    for k in range(pick_rows.shape[1] // LANES):
        source = spread(pick_rows[0:1, k * LANES : (k + 1) * LANES], 8)
        value = jnp.where(tile == k, lane_take(source, place), value)
    pick[...] = value


def fringe_own(slot_ref, remote, own):
    lane = lax.broadcasted_iota(jnp.int32, (8, LANES), 1)
    for v in range(5):
        value = slot_ref[0, 0, v, 0:8, :]
        for k in range(6):
            for block in range(4):
                start = 24 * block + 4 * k
                source = slot_ref[k // 3, k % 3, v, 8 * block : 8 * block + 8, :]
                source = pltpu.roll(source, (start - remote) % LANES, axis=1)
                value = jnp.where((lane >= start) & (lane < start + 4), source, value)
        own[v] = value


def inner_jumps(remote, slot_ref, partner, scale_ref, inverse, jump):
    shared = lax.broadcasted_iota(jnp.int32, (ROWS, LANES), 1) < remote
    for d in range(3):
        high = [slot_ref[0, d, v] for v in range(5)]
        low = [slot_ref[1, d, v] for v in range(5)]

        def other(side, own):
            starts = [((side * 3 + d) * 5 + v) * ROWS for v in range(5)]
            return [jnp.where(shared, partner[s : s + ROWS, :], o) for s, o in zip(starts, own)]

        scale = spread(scale_ref[d : d + 1, :], ROWS)
        for side, value in (
            (0, common(high, other(1, low), d)),
            (1, common(other(0, high), low, d)),
        ):
            back = jnp.concatenate([inverse[side * 3 + d]] * 4, axis=0)
            start = (side * 3 + d) * ROWS
            for v in range(5):
                jump[v, start : start + ROWS, :] = lane_take(value[v], back) * scale


def fringe_jumps(remote, each, pick, own, by_grid, scale_ref, inverse, jump, factor):
    grids = by_grid.shape[0]
    chosen = pick[...]
    owner, place = chosen // each, chosen - each * (chosen // each)
    outside = [None] * 5
    for g in range(grids):
        for v in range(5):
            source = lane_take(spread(by_grid[g, v : v + 1, :], 8), place)
            outside[v] = source if g == 0 else jnp.where(owner == g, source, outside[v])
    inside = [own[v] for v in range(5)]
    lane = lax.broadcasted_iota(jnp.int32, (8, LANES), 1)
    face = lane // 4 - 6 * (lane // 24)
    d = face - 3 * (face // 3)
    normal = [d == n for n in range(3)]
    sign = jnp.where(face < 3, 0.5, -0.5)
    outer_flux, outer_wave = lane_euler(outside, normal)
    inner_flux, inner_wave = lane_euler(inside, normal)
    wave = sign * jnp.maximum(outer_wave, inner_wave)
    value = [
        0.5 * (a + b) - wave * (o - i)
        for a, b, o, i in zip(outer_flux, inner_flux, outside, inside)
    ]
    for v in range(5):
        for k in range(6):
            slot = inverse[k] - remote
            here = (slot >= 0) & (slot < FRP)
            slot = jnp.where(here, slot, 0) + 4 * k
            scale = spread(scale_ref[k % 3 : k % 3 + 1, :], 8)
            blocks = []
            for block in range(4):
                start = k * ROWS + 8 * block
                new = lane_take(value[v], slot + 24 * block) * scale
                blocks.append(jnp.where(here, new, jump[v, start : start + 8, :]))
            store_parts(factor, k * ROWS, v, jnp.concatenate(blocks, axis=0))


def ring_distance(offset, size):
    return min(offset, size - offset)


def kernel(grids, parts, *refs):
    inputs, (out_ref,), buffers, scratch = refs[:10], refs[10:11], refs[11:21], refs[21:]
    (state_ref, scale_ref, plus_ref, minus_ref, cell_ref, weight_ref, pick_ref) = buffers[:7]
    face_ref, volume_ref, lift_ref = buffers[7:]
    (
        points, pair_weight, weight, donor, slot, message, partner_in, outgoing, incoming, relay,
        face_factor, flux, lift_factor, total, inverse, pick_rows, pick, own, partner, jump, by_grid,
        load_sem, sends, recvs, entered,
    ) = scratch
    loads = [
        pltpu.make_async_copy(source, target, load_sem.at[n])
        for n, (source, target) in enumerate(zip(inputs, buffers))
    ]
    for n in (0, 4, 5):
        loads[n].start()
    grid = lax.axis_index("grid")
    part = lax.axis_index("dom")
    across = 4 if parts % 4 == 0 else 1
    down = parts // across
    z, x = part // across, lax.rem(part, across)
    along_z = [lax.rem(z + k, down) * across for k in range(down)]
    along_x = [lax.rem(x + k, across) for k in range(across)]
    chips = grids // 2
    assert chips in (1, 2, 4, 8)
    core = lax.rem(grid, 2)
    along_y = [lax.rem(grid // 2 + k, chips) * 2 for k in range(chips)]

    def part_at(k):
        return along_z[k // across] + along_x[k % across]

    def cores_at(k):
        other = along_y[k] + 1 - core
        return [along_y[k] + core, other] if k else [other]

    chip_steps = sorted(range(chips), key=lambda k: -ring_distance(k, chips))
    part_steps = sorted(
        range(1, parts),
        key=lambda k: -(ring_distance(k // across, down) + ring_distance(k % across, across)),
    )
    near = [peer for k in chip_steps if ring_distance(k, chips) <= 2 for peer in cores_at(k)]
    relays = sorted({2 % chips, -2 % chips} - {0})
    barrier = pltpu.get_barrier_semaphore()
    for k in part_steps:
        pl.semaphore_signal(barrier, inc=1, device_id=(grid, part_at(k)), device_id_type=MESH)
    for peer in near:
        pl.semaphore_signal(barrier, inc=1, device_id=(peer, part), device_id_type=MESH)
    for n in (2, 3, 7, 1, 6, 8, 9):
        loads[n].start()

    def send(n, source, place, target, mine, to_grid, to_part):
        pltpu.make_async_remote_copy(
            src_ref=source.at[place], dst_ref=target.at[mine],
            send_sem=sends.at[n], recv_sem=recvs.at[n],
            device_id=(to_grid, to_part), device_id_type=MESH,
        ).start()

    def finish(semaphore, buffer, count):
        whole = buffer.at[pl.ds(0, count)]
        pltpu.make_async_copy(whole, whole, semaphore).wait()

    loads[0].wait()
    load_state(state_ref, points)
    loads[4].wait()
    loads[5].wait()
    for tile in range(cell_ref.shape[-1] // LANES):
        donor_tile(
            tile, points, cell_ref, weight_ref, pair_weight.at[tile % 2], weight.at[tile % 2], donor
        )
    turned = donor[...].reshape(grids * 8, LANES)
    turned = jnp.concatenate([turned] * (LANES // (grids * 8)), axis=0).T
    each = outgoing.shape[0] * outgoing.shape[1]
    outgoing[...] = turned[0:each].reshape(outgoing.shape)
    pl.semaphore_wait(barrier, parts - 1 + len(near))
    for k in part_steps:
        peer = part_at(k)
        send(0, outgoing, peer, incoming, part, grid, peer)
    for k in relays:
        pl.semaphore_signal(
            entered, inc=1, device_id=(along_y[k] + core, part), device_id_type=MESH
        )
    incoming[part] = outgoing[part]

    for n in (2, 3, 7):
        loads[n].wait()
    face_slots(points, plus_ref, minus_ref, face_ref, face_factor, slot)
    face_messages(slot, message)
    mine = pl.ds(pl.multiple_of(part * 8, 8), 8)
    for k in part_steps:
        peer = part_at(k)
        send(1, message, pl.ds(pl.multiple_of(peer * 8, 8), 8), partner_in, mine, grid, peer)
    partner_in[mine, :] = message[mine, :]

    for n in (1, 6, 8, 9):
        loads[n].wait()
    volume_terms(points, scale_ref, volume_ref, flux, total)
    inverse_orders(plus_ref, minus_ref, inverse)
    fringe_picks(pick_ref, pick_rows, pick)
    fringe_own(slot, parts, own)

    finish(recvs.at[0], incoming, parts - 1)
    turned = incoming[...].reshape(each, LANES)
    turned = jnp.concatenate([turned] * (LANES // each), axis=0).T
    relay[...] = turned[0 : grids * 8].reshape(relay.shape)
    if relays:
        pl.semaphore_wait(entered, len(relays))
    for k in chip_steps:
        for peer in cores_at(k):
            send(2, relay, peer, by_grid, grid, peer, part)
    by_grid[grid] = relay[grid]

    finish(recvs.at[1], partner_in, 8 * (parts - 1))
    partner_faces(partner_in, partner)
    inner_jumps(parts, slot, partner, scale_ref, inverse, jump)
    finish(sends.at[0], outgoing, parts - 1)
    finish(sends.at[1], message, 8 * (parts - 1))
    finish(sends.at[2], relay, grids - 1)

    finish(recvs.at[2], by_grid, grids - 1)
    fringe_jumps(parts, each, pick, own, by_grid, scale_ref, inverse, jump, lift_factor)
    for v, value in products(lift_ref, lift_factor):
        out_ref[v] = (total[v] + value)[0:125]


def body(grids, parts, state, scales, plus, minus, cell, weights, picks):
    f32, i32 = jnp.float32, jnp.int32
    total_slots = cell.shape[-1]
    slots = total_slots // (grids * parts)
    weights = jnp.transpose(weights, (1, 2, 0, 3))
    inputs = (state, scales, plus, minus, cell, weights, picks) + matrices()
    pick_tiles = -(-picks.shape[-1] // LANES)
    return pl.pallas_call(
        functools.partial(kernel, grids, parts),
        out_shape=jax.ShapeDtypeStruct(state.shape, f32),
        in_specs=[pl.BlockSpec(memory_space=pltpu.HBM)] * len(inputs),
        out_specs=pl.BlockSpec(memory_space=pltpu.VMEM),
        scratch_shapes=[pltpu.VMEM(x.shape, x.dtype) for x in inputs]
        + [
            pltpu.VMEM((5, LANES, LANES), f32),
            pltpu.VMEM((2, 32, LANES), f32),
            pltpu.VMEM((2, LANES, LANES), f32),
            pltpu.VMEM((grids, 8, LANES), f32),
            pltpu.VMEM((2, 3, 5, ROWS, LANES), f32),
            pltpu.VMEM((parts * 8, LANES), f32),
            pltpu.VMEM((parts * 8, LANES), f32),
            pltpu.VMEM((parts, slots, LANES), f32),
            pltpu.VMEM((parts, slots, LANES), f32),
            pltpu.VMEM((grids, 8, LANES), f32),
            pltpu.VMEM((3 * LANES, 5 * LANES), jnp.bfloat16),
            pltpu.VMEM((9 * LANES, 5 * LANES), jnp.bfloat16),
            pltpu.VMEM((18 * ROWS, 5 * LANES), jnp.bfloat16),
            pltpu.VMEM((5, LANES, LANES), f32),
            pltpu.VMEM((6, 8, LANES), i32),
            pltpu.VMEM((8, pick_tiles * LANES), i32),
            pltpu.VMEM((8, LANES), i32),
            pltpu.VMEM((5, 8, LANES), f32),
            pltpu.VMEM((8 * LANES, LANES), f32),
            pltpu.VMEM((5, 6 * ROWS, LANES), f32),
            pltpu.VMEM((grids, 8, LANES), f32),
            pltpu.SemaphoreType.DMA((len(inputs),)),
            pltpu.SemaphoreType.DMA((3,)),
            pltpu.SemaphoreType.DMA((3,)),
            pltpu.SemaphoreType.REGULAR,
        ],
        compiler_params=pltpu.CompilerParams(
            collective_id=0, has_side_effects=True, vmem_limit_bytes=24 * 1024 * 1024
        ),
        name="step",
    )(*(pltpu.with_memory_space_constraint(x, pltpu.HBM) for x in inputs))


def solution(mesh):
    both = ("grid", "dom")
    return jax.shard_map(
        functools.partial(body, mesh.shape["grid"], mesh.shape["dom"]),
        mesh=mesh,
        in_specs=(
            P(None, None, both),
            P(None, both),
            P(None, both),
            P(None, both),
            P(both, None),
            P(both, None, None, None),
            P(both, None),
        ),
        out_specs=P(None, None, both),
        check_vma=False,
    )
```

```python
import functools
import math

import jax
import jax.numpy as jnp
import numpy as np
from jax import lax
from jax.experimental import pallas as pl
from jax.experimental.pallas import tpu as pltpu
from jax.sharding import PartitionSpec as P

MESH = pl.DeviceIdType.MESH
LANES = 128
ROWS = 32
FRP = 4
ACROSS = 4


def gauss_nodes():
    outer = math.sqrt(5.0 + 2.0 * math.sqrt(10.0 / 7.0)) / 3.0
    inner = math.sqrt(5.0 - 2.0 * math.sqrt(10.0 / 7.0)) / 3.0
    return [-outer, -inner, 0.0, inner, outer]


def basis_value(nodes, column, x):
    value = 1.0
    for other in range(5):
        if other != column:
            value = value * (x - nodes[other]) / (nodes[column] - nodes[other])
    return value


def basis_slope(nodes, column, x):
    total = 0.0
    for skipped in range(5):
        if skipped != column:
            value = 1.0 / (nodes[column] - nodes[skipped])
            for other in range(5):
                if other != column and other != skipped:
                    value = value * (x - nodes[other]) / (nodes[column] - nodes[other])
            total = total + value
    return total


def legendre_slopes(x):
    values = [1.0, x]
    slopes = [0.0, 1.0]
    for order in range(1, 5):
        values.append(((2 * order + 1) * x * values[order] - order * values[order - 1]) / (order + 1))
        slopes.append(slopes[order - 1] + (2 * order + 1) * values[order])
    return slopes[4], slopes[5]


def split_point(p, direction):
    index = [p // 25, p // 5 % 5, p % 5]
    along = index.pop(direction)
    return along, 5 * index[0] + index[1]


def split_constant(matrix):
    high = matrix.astype(jnp.bfloat16)
    low = (matrix - high.astype(np.float32)).astype(jnp.bfloat16)
    return jnp.asarray(np.concatenate([high, high, low], axis=1))


def matrices():
    nodes = gauss_nodes()
    deriv = np.array([[basis_slope(nodes, m, x) for m in range(5)] for x in nodes])
    lower = np.array([basis_value(nodes, m, -1.0) for m in range(5)])
    upper = np.array([basis_value(nodes, m, 1.0) for m in range(5)])
    slopes = [legendre_slopes(x) for x in nodes]
    lift_low = np.array([-0.5 * (five - four) for four, five in slopes])
    lift_high = np.array([0.5 * (five + four) for four, five in slopes])
    folded = deriv - np.outer(lift_low, lower) - np.outer(lift_high, upper)
    faces = np.zeros((2, 3, ROWS, LANES))
    volume = np.zeros((LANES, 3, LANES))
    lift = np.zeros((LANES, 2, 3, ROWS))
    for direction in range(3):
        for p in range(125):
            i, t = split_point(p, direction)
            faces[0, direction, t, p] = upper[i]
            faces[1, direction, t, p] = lower[i]
            lift[p, 0, direction, t] = -lift_high[i]
            lift[p, 1, direction, t] = -lift_low[i]
            for other in range(125):
                m, s = split_point(other, direction)
                if s == t:
                    volume[p, direction, other] = -folded[i, m]
    faces[:, :, 25:] = faces[:, :, :1]
    return tuple(
        split_constant(m.astype(np.float32))
        for m in (
            faces.reshape(6 * ROWS, LANES),
            volume.reshape(LANES, 3 * LANES),
            lift.reshape(LANES, 6 * ROWS),
        )
    )


def lane_take(x, index):
    return jnp.take_along_axis(x, index, axis=1, mode="promise_in_bounds")


def spread(row, rows):
    return jnp.broadcast_to(row, (rows, row.shape[-1]))


def store_parts(ref, start, v, value):
    third = ref.shape[0] // 3
    rows, lanes = value.shape[0], slice(v * LANES, (v + 1) * LANES)
    high = value.astype(jnp.bfloat16)
    ref[start : start + rows, lanes] = high
    ref[third + start : third + start + rows, lanes] = (value - high.astype(jnp.float32)).astype(jnp.bfloat16)
    ref[2 * third + start : 2 * third + start + rows, lanes] = high


def products(constant_ref, ref):
    for v in range(0, 5, 2):
        width = min(2, 5 - v) * LANES
        block = jnp.dot(
            constant_ref[...], ref[:, v * LANES : v * LANES + width], preferred_element_type=jnp.float32
        )
        for k in range(width // LANES):
            yield v + k, block[:, k * LANES : (k + 1) * LANES]


def pressure_of(w, inverse):
    square = w[1] * w[1] + w[2] * w[2] + w[3] * w[3]
    return 0.4 * (w[4] - 0.5 * square * inverse)


def euler(w, direction):
    inverse = 1.0 / w[0]
    speed = w[1 + direction] * inverse
    pressure = pressure_of(w, inverse)
    flux = [w[1 + direction]] + [m * speed for m in w[1:4]] + [(w[4] + pressure) * speed]
    flux[1 + direction] = flux[1 + direction] + (pressure - 1.0)
    return flux, jnp.abs(speed) + jnp.sqrt(1.4 * pressure * inverse)


def common(left, right, direction):
    left_flux, left_wave = euler(left, direction)
    right_flux, right_wave = euler(right, direction)
    wave = jnp.maximum(left_wave, right_wave)
    return [
        0.5 * (lf + rf) - 0.5 * wave * (r - l)
        for lf, rf, l, r in zip(left_flux, right_flux, left, right)
    ]


def lane_euler(w, normal):
    inverse = 1.0 / w[0]
    momentum = jnp.where(normal[0], w[1], jnp.where(normal[1], w[2], w[3]))
    speed = momentum * inverse
    pressure = pressure_of(w, inverse)
    flux = [momentum] + [
        w[1 + d] * speed + jnp.where(normal[d], pressure - 1.0, 0.0) for d in range(3)
    ]
    flux.append((w[4] + pressure) * speed)
    return flux, jnp.abs(speed) + jnp.sqrt(1.4 * pressure * inverse)


def load_state(state_ref, points):
    for v in range(5):
        points[v, 0:120, :] = state_ref[v, 0:120, :]
        points[v, 120:125, :] = state_ref[v, 120:125, :]
        points[v, 125:128, :] = state_ref[v, 122:125, :]


def row_choice(row, values, index):
    value = values[index[-1]]
    for s in range(len(index) - 2, -1, -1):
        if index[s] != index[s + 1]:
            value = jnp.where(row <= s, values[index[s]], value)
    return value


def donor_tile(tile, points, cell_ref, weight_ref, donor_ref):
    per_tile = LANES * donor_ref.shape[0] // cell_ref.shape[-1]
    lanes = pl.ds(pl.multiple_of(tile * LANES, LANES), LANES)
    row = lax.broadcasted_iota(jnp.int32, (8, LANES), 0)
    turn = row - 5 * (row // 5)
    along = [[spread(weight_ref[d, k, :, lanes], 8) for k in range(5)] for d in range(3)]
    last = []
    for start in range(5):
        value = along[2][(start + 4) % 5]
        for k in range(4):
            value = jnp.where(turn == k, along[2][(start + k) % 5], value)
        last.append(value)
    index = spread(cell_ref[0:1, lanes], 8)
    sums = [None] * 5
    for k in range(LANES // 8):
        number = [min(8 * k + s, 124) for s in range(8)]
        scale = row_choice(row, along[0], [p // 25 for p in number])
        pairs = [p // 5 for p in number]
        middle = row_choice(row, [along[1][p % 5] for p in range(25)], pairs)
        scale = scale * middle * last[8 * k % 5]
        if 8 * k + 8 > 125:
            scale = jnp.where(row < 125 - 8 * k, scale, 0.0)
        for v in range(5):
            term = lane_take(points[v, 8 * k : 8 * k + 8, :], index) * scale
            sums[v] = term if k == 0 else sums[v] + term
    value = jnp.zeros((8, LANES), jnp.float32)
    for v in range(5):
        value = jnp.where(row == v, jnp.sum(sums[v], axis=0, keepdims=True), value)
    donor_ref[tile * per_tile] = value
    for k in range(1, per_tile):
        donor_ref[tile * per_tile + k] = pltpu.roll(value, LANES - k * (LANES // per_tile), axis=1)


def face_slots(points, plus_ref, minus_ref, face_ref, factor, slot_ref):
    centre = (1.0, 0.0, 0.0, 0.0, 2.5)
    for v in range(5):
        store_parts(factor, 0, v, points[v] - centre[v])
    for v, faces in products(face_ref, factor):
        for side, order in ((0, plus_ref), (1, minus_ref)):
            for d in range(3):
                start = (side * 3 + d) * ROWS
                slot_ref[side, d, v] = centre[v] + lane_take(
                    faces[start : start + ROWS], spread(order[d : d + 1, :], ROWS)
                )


def face_messages(slot_ref, message_ref):
    count = message_ref.shape[0] // 8
    for row in range(8):
        columns = [
            slot_ref[n // 15, n // 5 % 3, n % 5] for n in range(4 * row, min(4 * row + 4, 30))
        ]
        columns += [columns[-1]] * (4 - len(columns))
        message_ref[pl.ds(row, count, stride=8), :] = jnp.concatenate(columns, axis=0).T[0:count]


def partner_faces(partner_in, partner):
    count = partner_in.shape[0] // 8
    for row in range(8):
        block = partner_in[pl.ds(row, count, stride=8), :]
        block = jnp.concatenate([block] * (LANES // count), axis=0).T
        partner[row * LANES : (row + 1) * LANES, :] = block


def volume_terms(points, scale_ref, volume_ref, flux, total):
    w = [points[v] for v in range(5)]
    for d in range(3):
        pieces = euler(w, d)[0]
        for v in range(5):
            store_parts(flux, d * LANES, v, pieces[v] * spread(scale_ref[d : d + 1, :], LANES))
    for v, value in products(volume_ref, flux):
        total[v] = value


def inverse_orders(plus_ref, minus_ref, inverse):
    element = lax.broadcasted_iota(jnp.int32, (LANES, LANES), 0)
    count = lax.broadcasted_iota(jnp.int32, (8, LANES), 1).astype(jnp.float32).astype(jnp.bfloat16)
    for side, order in ((0, plus_ref), (1, minus_ref)):
        for d in range(3):
            chosen = element == spread(order[d : d + 1, :], LANES)
            chosen = jnp.where(chosen, 1.0, 0.0).astype(jnp.bfloat16)
            inverse[side * 3 + d] = lax.dot_general(
                count, chosen, (((1,), (1,)), ((), ())), preferred_element_type=jnp.float32
            ).astype(jnp.int32)


def fringe_picks(pick_ref, pick_rows, pick):
    pick_rows[...] = jnp.zeros(pick_rows.shape, jnp.int32)
    pick_rows[0:1, 0 : pick_ref.shape[1]] = pick_ref[...]
    row = lax.broadcasted_iota(jnp.int32, (8, LANES), 0)
    lane = lax.broadcasted_iota(jnp.int32, (8, LANES), 1)
    block, face = lane // 24, lane // 4 - 6 * (lane // 24)
    side, d = face // 3, face - 3 * (face // 3)
    t = jnp.minimum(8 * block + row, 24)
    number = ((2 * d + 1 - side) * 25 + t) * FRP + lane - 4 * (lane // 4)
    tile, place = number // LANES, number - LANES * (number // LANES)
    value = jnp.zeros((8, LANES), jnp.int32)
    for k in range(pick_rows.shape[1] // LANES):
        source = spread(pick_rows[0:1, k * LANES : (k + 1) * LANES], 8)
        value = jnp.where(tile == k, lane_take(source, place), value)
    pick[...] = value


def fringe_own(slot_ref, remote, own):
    lane = lax.broadcasted_iota(jnp.int32, (8, LANES), 1)
    for v in range(5):
        value = slot_ref[0, 0, v, 0:8, :]
        for k in range(6):
            for block in range(4):
                start = 24 * block + 4 * k
                source = slot_ref[k // 3, k % 3, v, 8 * block : 8 * block + 8, :]
                source = pltpu.roll(source, (start - remote) % LANES, axis=1)
                value = jnp.where((lane >= start) & (lane < start + 4), source, value)
        own[v] = value


def inner_jumps(remote, slot_ref, partner, scale_ref, inverse, jump):
    shared = lax.broadcasted_iota(jnp.int32, (ROWS, LANES), 1) < remote
    for d in range(3):
        high = [slot_ref[0, d, v] for v in range(5)]
        low = [slot_ref[1, d, v] for v in range(5)]

        def other(side, own):
            starts = [((side * 3 + d) * 5 + v) * ROWS for v in range(5)]
            return [jnp.where(shared, partner[s : s + ROWS, :], o) for s, o in zip(starts, own)]

        scale = spread(scale_ref[d : d + 1, :], ROWS)
        for side, value in (
            (0, common(high, other(1, low), d)),
            (1, common(other(0, high), low, d)),
        ):
            back = jnp.concatenate([inverse[side * 3 + d]] * 4, axis=0)
            start = (side * 3 + d) * ROWS
            for v in range(5):
                jump[v, start : start + ROWS, :] = lane_take(value[v], back) * scale


def fringe_jumps(remote, arrived_ref, pick, own, by_grid, scale_ref, inverse, jump, factor):
    parts, slots, width = arrived_ref.shape
    grids = by_grid.shape[0]
    each = parts * slots
    turned = arrived_ref[...].reshape(each, width)
    turned = jnp.concatenate([turned] * (LANES // each), axis=0).T
    by_grid[...] = turned[0 : grids * 8].reshape(grids, 8, LANES)
    chosen = pick[...]
    owner, place = chosen // each, chosen - each * (chosen // each)
    outside = [None] * 5
    for g in range(grids):
        for v in range(5):
            source = lane_take(spread(by_grid[g, v : v + 1, :], 8), place)
            outside[v] = source if g == 0 else jnp.where(owner == g, source, outside[v])
    inside = [own[v] for v in range(5)]
    lane = lax.broadcasted_iota(jnp.int32, (8, LANES), 1)
    face = lane // 4 - 6 * (lane // 24)
    d = face - 3 * (face // 3)
    normal = [d == n for n in range(3)]
    sign = jnp.where(face < 3, 0.5, -0.5)
    outer_flux, outer_wave = lane_euler(outside, normal)
    inner_flux, inner_wave = lane_euler(inside, normal)
    wave = sign * jnp.maximum(outer_wave, inner_wave)
    value = [
        0.5 * (a + b) - wave * (o - i)
        for a, b, o, i in zip(outer_flux, inner_flux, outside, inside)
    ]
    for v in range(5):
        for k in range(6):
            slot = inverse[k] - remote
            here = (slot >= 0) & (slot < FRP)
            slot = jnp.where(here, slot, 0) + 4 * k
            scale = spread(scale_ref[k % 3 : k % 3 + 1, :], 8)
            blocks = []
            for block in range(4):
                start = k * ROWS + 8 * block
                new = lane_take(value[v], slot + 24 * block) * scale
                blocks.append(jnp.where(here, new, jump[v, start : start + 8, :]))
            store_parts(factor, k * ROWS, v, jnp.concatenate(blocks, axis=0))


def ring_distance(offset, size):
    return min(offset, size - offset)


def kernel(grids, parts, *refs):
    inputs, (out_ref,), buffers, scratch = refs[:10], refs[10:11], refs[11:21], refs[21:]
    (state_ref, scale_ref, plus_ref, minus_ref, cell_ref, weight_ref, pick_ref) = buffers[:7]
    face_ref, volume_ref, lift_ref = buffers[7:]
    (
        points, donor, slot, message, partner_in, gathered, relay, arrived,
        face_factor, flux, lift_factor, total, inverse, pick_rows, pick, own, partner, jump, by_grid,
        load_sem, sends, recvs, entered,
    ) = scratch
    loads = [
        pltpu.make_async_copy(source, target, load_sem.at[n])
        for n, (source, target) in enumerate(zip(inputs, buffers))
    ]
    for n in (0, 4, 5):
        loads[n].start()
    grid = lax.axis_index("grid")
    part = lax.axis_index("dom")
    across, down = ACROSS, parts // ACROSS
    half = down // 2
    z, x = part // across, lax.rem(part, across)
    along_x = [lax.rem(x + k, across) for k in range(across)]
    along_grid = [lax.rem(grid + k, grids) for k in range(grids)]
    row_peers = [z * across + k for k in along_x[1:]]

    def for_lower(act):
        for k in range(down - 1, 0, -1):
            @pl.when(z >= k)
            def _(k=k):
                for column in along_x:
                    act((z - k) * across + column)

    def for_higher(act, low, high):
        for k in range(1, down):
            @pl.when((z + k >= low) & (z + k < high))
            def _(k=k):
                for column in along_x:
                    act((z + k) * across + column)

    barrier = pltpu.get_barrier_semaphore()

    def enter(peer):
        pl.semaphore_signal(barrier, inc=1, device_id=(grid, peer), device_id_type=MESH)

    for k in sorted(range(1, grids), key=lambda k: -ring_distance(k, grids)):
        pl.semaphore_signal(barrier, inc=1, device_id=(along_grid[k], part), device_id_type=MESH)
    for peer in row_peers:
        enter(peer)
    for_higher(enter, 0, down)
    for n in (2, 3, 7, 1, 6, 8, 9):
        loads[n].start()

    def send(n, source, place, target, mine, to_grid, to_part):
        pltpu.make_async_remote_copy(
            src_ref=source.at[place], dst_ref=target.at[mine],
            send_sem=sends.at[n], recv_sem=recvs.at[n],
            device_id=(to_grid, to_part), device_id_type=MESH,
        ).start()

    def finish(semaphore, buffer, count):
        whole = buffer.at[pl.ds(0, count)]
        pltpu.make_async_copy(whole, whole, semaphore).wait()

    loads[0].wait()
    load_state(state_ref, points)
    loads[4].wait()
    loads[5].wait()
    def told(peer):
        group = entered.at[z // max(half, 1)] if half else entered.at[0]
        pl.semaphore_signal(group, inc=1, device_id=(grid, peer), device_id_type=MESH)

    tiles = cell_ref.shape[-1] // LANES
    per_tile = grids // tiles
    near = grid // per_tile
    for n, step in enumerate(sorted(range(tiles), key=lambda k: -ring_distance(k, tiles))):
        tile = lax.rem(near + step, tiles)
        donor_tile(tile, points, cell_ref, weight_ref, donor)
        if n == 0:
            pl.semaphore_wait(barrier, grids - 1 + across * (z + 1) - 1)
        for k in range(per_tile if step else per_tile - 1):
            first = lax.rem(grid, per_tile) + 1 if step == 0 else 0
            peer = tile * per_tile + lax.rem(first + k, per_tile)
            send(0, donor, peer, gathered, grid, peer, part)
        if n == 0:
            for_lower(told)
    gathered[grid] = donor[grid]

    for n in (2, 3, 7):
        loads[n].wait()
    face_slots(points, plus_ref, minus_ref, face_ref, face_factor, slot)
    face_messages(slot, message)
    mine = pl.ds(pl.multiple_of(part * 8, 8), 8)

    def send_faces(peer):
        send(1, message, pl.ds(pl.multiple_of(peer * 8, 8), 8), partner_in, mine, grid, peer)

    for_lower(send_faces)
    for peer in row_peers:
        send_faces(peer)
    partner_in[mine, :] = message[mine, :]

    for n in (1, 6, 8, 9):
        loads[n].wait()
    volume_terms(points, scale_ref, volume_ref, flux, total)
    inverse_orders(plus_ref, minus_ref, inverse)
    fringe_picks(pick_ref, pick_rows, pick)
    fringe_own(slot, parts, own)

    finish(recvs.at[0], gathered, grids - 1)
    turned = gathered[...].reshape(grids * 8, LANES)
    if grids * 8 < LANES:
        turned = jnp.concatenate([turned] * (LANES // (grids * 8)), axis=0)
    relay[...] = turned.T[0 : relay.shape[0] * relay.shape[1]].reshape(relay.shape)
    def send_donors(peer):
        send(2, relay, peer, arrived, part, grid, peer)

    def send_both(peer):
        send_donors(peer)
        send_faces(peer)

    for_lower(send_donors)
    for peer in row_peers:
        send_donors(peer)
    arrived[part] = relay[part]
    for group, low, high in ((0, 0, half), (1, half, down)):
        later = across * jnp.maximum(high - jnp.maximum(z + 1, low), 0)

        @pl.when(later > 0)
        def _():
            pl.semaphore_wait(entered.at[group], later)
            for_higher(send_both, low, high)

    finish(recvs.at[1], partner_in, 8 * (parts - 1))
    partner_faces(partner_in, partner)
    inner_jumps(parts, slot, partner, scale_ref, inverse, jump)
    finish(sends.at[0], donor, grids - 1)
    finish(sends.at[1], message, 8 * (parts - 1))
    finish(sends.at[2], relay, parts - 1)

    finish(recvs.at[2], arrived, parts - 1)
    fringe_jumps(parts, arrived, pick, own, by_grid, scale_ref, inverse, jump, lift_factor)
    for v, value in products(lift_ref, lift_factor):
        out_ref[v] = (total[v] + value)[0:125]


def body(grids, parts, state, scales, plus, minus, cell, weights, picks):
    f32, i32 = jnp.float32, jnp.int32
    total_slots = cell.shape[-1]
    slots = total_slots // (grids * parts)
    weights = jnp.transpose(weights, (1, 2, 0, 3))
    inputs = (state, scales, plus, minus, cell, weights, picks) + matrices()
    pick_tiles = -(-picks.shape[-1] // LANES)
    return pl.pallas_call(
        functools.partial(kernel, grids, parts),
        out_shape=jax.ShapeDtypeStruct(state.shape, f32),
        in_specs=[pl.BlockSpec(memory_space=pltpu.HBM)] * len(inputs),
        out_specs=pl.BlockSpec(memory_space=pltpu.VMEM),
        scratch_shapes=[pltpu.VMEM(x.shape, x.dtype) for x in inputs]
        + [
            pltpu.VMEM((5, LANES, LANES), f32),
            pltpu.VMEM((grids, 8, LANES), f32),
            pltpu.VMEM((2, 3, 5, ROWS, LANES), f32),
            pltpu.VMEM((parts * 8, LANES), f32),
            pltpu.VMEM((parts * 8, LANES), f32),
            pltpu.VMEM((grids, 8, LANES), f32),
            pltpu.VMEM((parts, slots, LANES), f32),
            pltpu.VMEM((parts, slots, LANES), f32),
            pltpu.VMEM((3 * LANES, 5 * LANES), jnp.bfloat16),
            pltpu.VMEM((9 * LANES, 5 * LANES), jnp.bfloat16),
            pltpu.VMEM((18 * ROWS, 5 * LANES), jnp.bfloat16),
            pltpu.VMEM((5, LANES, LANES), f32),
            pltpu.VMEM((6, 8, LANES), i32),
            pltpu.VMEM((8, pick_tiles * LANES), i32),
            pltpu.VMEM((8, LANES), i32),
            pltpu.VMEM((5, 8, LANES), f32),
            pltpu.VMEM((8 * LANES, LANES), f32),
            pltpu.VMEM((5, 6 * ROWS, LANES), f32),
            pltpu.VMEM((grids, 8, LANES), f32),
            pltpu.SemaphoreType.DMA((len(inputs),)),
            pltpu.SemaphoreType.DMA((3,)),
            pltpu.SemaphoreType.DMA((3,)),
            pltpu.SemaphoreType.REGULAR((2,)),
        ],
        compiler_params=pltpu.CompilerParams(
            collective_id=0, has_side_effects=True, vmem_limit_bytes=24 * 1024 * 1024
        ),
        name="step",
    )(*(pltpu.with_memory_space_constraint(x, pltpu.HBM) for x in inputs))


def solution(mesh):
    both = ("grid", "dom")
    return jax.shard_map(
        functools.partial(body, mesh.shape["grid"], mesh.shape["dom"]),
        mesh=mesh,
        in_specs=(
            P(None, None, both),
            P(None, both),
            P(None, both),
            P(None, both),
            P(both, None),
            P(both, None, None, None),
            P(both, None),
        ),
        out_specs=P(None, None, both),
        check_vma=False,
    )
```

```python
import functools
import math

import jax
import jax.numpy as jnp
import numpy as np
from jax import lax
from jax.experimental import pallas as pl
from jax.experimental.pallas import tpu as pltpu
from jax.sharding import PartitionSpec as P

MESH = pl.DeviceIdType.MESH
LANES = 128
ROWS = 32
FRP = 4
ACROSS = 4


def gauss_nodes():
    outer = math.sqrt(5.0 + 2.0 * math.sqrt(10.0 / 7.0)) / 3.0
    inner = math.sqrt(5.0 - 2.0 * math.sqrt(10.0 / 7.0)) / 3.0
    return [-outer, -inner, 0.0, inner, outer]


def basis_value(nodes, column, x):
    value = 1.0
    for other in range(5):
        if other != column:
            value = value * (x - nodes[other]) / (nodes[column] - nodes[other])
    return value


def basis_slope(nodes, column, x):
    total = 0.0
    for skipped in range(5):
        if skipped != column:
            value = 1.0 / (nodes[column] - nodes[skipped])
            for other in range(5):
                if other != column and other != skipped:
                    value = value * (x - nodes[other]) / (nodes[column] - nodes[other])
            total = total + value
    return total


def legendre_slopes(x):
    values = [1.0, x]
    slopes = [0.0, 1.0]
    for order in range(1, 5):
        values.append(((2 * order + 1) * x * values[order] - order * values[order - 1]) / (order + 1))
        slopes.append(slopes[order - 1] + (2 * order + 1) * values[order])
    return slopes[4], slopes[5]


def split_point(p, direction):
    index = [p // 25, p // 5 % 5, p % 5]
    along = index.pop(direction)
    return along, 5 * index[0] + index[1]


def split_constant(matrix):
    high = matrix.astype(jnp.bfloat16)
    low = (matrix - high.astype(np.float32)).astype(jnp.bfloat16)
    return jnp.asarray(np.concatenate([high, high, low], axis=1))


def matrices():
    nodes = gauss_nodes()
    deriv = np.array([[basis_slope(nodes, m, x) for m in range(5)] for x in nodes])
    lower = np.array([basis_value(nodes, m, -1.0) for m in range(5)])
    upper = np.array([basis_value(nodes, m, 1.0) for m in range(5)])
    slopes = [legendre_slopes(x) for x in nodes]
    lift_low = np.array([-0.5 * (five - four) for four, five in slopes])
    lift_high = np.array([0.5 * (five + four) for four, five in slopes])
    folded = deriv - np.outer(lift_low, lower) - np.outer(lift_high, upper)
    faces = np.zeros((2, 3, ROWS, LANES))
    volume = np.zeros((LANES, 3, LANES))
    lift = np.zeros((LANES, 2, 3, ROWS))
    for direction in range(3):
        for p in range(125):
            i, t = split_point(p, direction)
            faces[0, direction, t, p] = upper[i]
            faces[1, direction, t, p] = lower[i]
            lift[p, 0, direction, t] = -lift_high[i]
            lift[p, 1, direction, t] = -lift_low[i]
            for other in range(125):
                m, s = split_point(other, direction)
                if s == t:
                    volume[p, direction, other] = -folded[i, m]
    faces[:, :, 25:] = faces[:, :, :1]
    return tuple(
        split_constant(m.astype(np.float32))
        for m in (
            faces.reshape(6 * ROWS, LANES),
            volume.reshape(LANES, 3 * LANES),
            lift.reshape(LANES, 6 * ROWS),
        )
    )


def lane_take(x, index):
    return jnp.take_along_axis(x, index, axis=1, mode="promise_in_bounds")


def spread(row, rows):
    return jnp.broadcast_to(row, (rows, row.shape[-1]))


def store_parts(ref, start, v, value):
    third = ref.shape[0] // 3
    rows, lanes = value.shape[0], slice(v * LANES, (v + 1) * LANES)
    high = value.astype(jnp.bfloat16)
    ref[start : start + rows, lanes] = high
    ref[third + start : third + start + rows, lanes] = (value - high.astype(jnp.float32)).astype(jnp.bfloat16)
    ref[2 * third + start : 2 * third + start + rows, lanes] = high


def products(constant_ref, ref):
    for v in range(0, 5, 2):
        width = min(2, 5 - v) * LANES
        block = jnp.dot(
            constant_ref[...], ref[:, v * LANES : v * LANES + width], preferred_element_type=jnp.float32
        )
        for k in range(width // LANES):
            yield v + k, block[:, k * LANES : (k + 1) * LANES]


def pressure_of(w, inverse):
    square = w[1] * w[1] + w[2] * w[2] + w[3] * w[3]
    return 0.4 * (w[4] - 0.5 * square * inverse)


def euler(w, direction):
    inverse = 1.0 / w[0]
    speed = w[1 + direction] * inverse
    pressure = pressure_of(w, inverse)
    flux = [w[1 + direction]] + [m * speed for m in w[1:4]] + [(w[4] + pressure) * speed]
    flux[1 + direction] = flux[1 + direction] + (pressure - 1.0)
    return flux, jnp.abs(speed) + jnp.sqrt(1.4 * pressure * inverse)


def common(left, right, direction):
    left_flux, left_wave = euler(left, direction)
    right_flux, right_wave = euler(right, direction)
    wave = jnp.maximum(left_wave, right_wave)
    return [
        0.5 * (lf + rf) - 0.5 * wave * (r - l)
        for lf, rf, l, r in zip(left_flux, right_flux, left, right)
    ]


def lane_euler(w, normal):
    inverse = 1.0 / w[0]
    momentum = jnp.where(normal[0], w[1], jnp.where(normal[1], w[2], w[3]))
    speed = momentum * inverse
    pressure = pressure_of(w, inverse)
    flux = [momentum] + [
        w[1 + d] * speed + jnp.where(normal[d], pressure - 1.0, 0.0) for d in range(3)
    ]
    flux.append((w[4] + pressure) * speed)
    return flux, jnp.abs(speed) + jnp.sqrt(1.4 * pressure * inverse)


def load_state(state_ref, points):
    for v in range(5):
        points[v, 0:120, :] = state_ref[v, 0:120, :]
        points[v, 120:125, :] = state_ref[v, 120:125, :]
        points[v, 125:128, :] = state_ref[v, 122:125, :]


def row_choice(row, values, index):
    value = values[index[-1]]
    for s in range(len(index) - 2, -1, -1):
        if index[s] != index[s + 1]:
            value = jnp.where(row <= s, values[index[s]], value)
    return value


def donor_tile(tile, points, cell_ref, weight_ref, donor_ref):
    per_tile = LANES * donor_ref.shape[0] // cell_ref.shape[-1]
    lanes = pl.ds(pl.multiple_of(tile * LANES, LANES), LANES)
    row = lax.broadcasted_iota(jnp.int32, (8, LANES), 0)
    turn = row - 5 * (row // 5)
    along = [[spread(weight_ref[d, k, :, lanes], 8) for k in range(5)] for d in range(3)]
    last = []
    for start in range(5):
        value = along[2][(start + 4) % 5]
        for k in range(4):
            value = jnp.where(turn == k, along[2][(start + k) % 5], value)
        last.append(value)
    index = spread(cell_ref[0:1, lanes], 8)
    sums = [None] * 5
    for k in range(LANES // 8):
        number = [min(8 * k + s, 124) for s in range(8)]
        scale = row_choice(row, along[0], [p // 25 for p in number])
        pairs = [p // 5 for p in number]
        middle = row_choice(row, [along[1][p % 5] for p in range(25)], pairs)
        scale = scale * middle * last[8 * k % 5]
        if 8 * k + 8 > 125:
            scale = jnp.where(row < 125 - 8 * k, scale, 0.0)
        for v in range(5):
            term = lane_take(points[v, 8 * k : 8 * k + 8, :], index) * scale
            sums[v] = term if k == 0 else sums[v] + term
    value = jnp.zeros((8, LANES), jnp.float32)
    for v in range(5):
        value = jnp.where(row == v, jnp.sum(sums[v], axis=0, keepdims=True), value)
    donor_ref[tile * per_tile] = value
    for k in range(1, per_tile):
        donor_ref[tile * per_tile + k] = pltpu.roll(value, LANES - k * (LANES // per_tile), axis=1)


def face_slots(points, plus_ref, minus_ref, face_ref, factor, slot_ref):
    centre = (1.0, 0.0, 0.0, 0.0, 2.5)
    for v in range(5):
        store_parts(factor, 0, v, points[v] - centre[v])
    for v, faces in products(face_ref, factor):
        for side, order in ((0, plus_ref), (1, minus_ref)):
            for d in range(3):
                start = (side * 3 + d) * ROWS
                slot_ref[side, d, v] = centre[v] + lane_take(
                    faces[start : start + ROWS], spread(order[d : d + 1, :], ROWS)
                )


def face_messages(slot_ref, message_ref):
    count = message_ref.shape[0] // 8
    for row in range(8):
        columns = [
            slot_ref[n // 15, n // 5 % 3, n % 5] for n in range(4 * row, min(4 * row + 4, 30))
        ]
        columns += [columns[-1]] * (4 - len(columns))
        message_ref[pl.ds(row, count, stride=8), :] = jnp.concatenate(columns, axis=0).T[0:count]


def partner_faces(partner_in, partner):
    count = partner_in.shape[0] // 8
    for row in range(8):
        block = partner_in[pl.ds(row, count, stride=8), :]
        block = jnp.concatenate([block] * (LANES // count), axis=0).T
        partner[row * LANES : (row + 1) * LANES, :] = block


def volume_terms(points, scale_ref, volume_ref, flux, total):
    w = [points[v] for v in range(5)]
    for d in range(3):
        pieces = euler(w, d)[0]
        for v in range(5):
            store_parts(flux, d * LANES, v, pieces[v] * spread(scale_ref[d : d + 1, :], LANES))
    for v, value in products(volume_ref, flux):
        total[v] = value


def inverse_orders(plus_ref, minus_ref, inverse):
    element = lax.broadcasted_iota(jnp.int32, (LANES, LANES), 0)
    count = lax.broadcasted_iota(jnp.int32, (8, LANES), 1).astype(jnp.float32).astype(jnp.bfloat16)
    for side, order in ((0, plus_ref), (1, minus_ref)):
        for d in range(3):
            chosen = element == spread(order[d : d + 1, :], LANES)
            chosen = jnp.where(chosen, 1.0, 0.0).astype(jnp.bfloat16)
            inverse[side * 3 + d] = lax.dot_general(
                count, chosen, (((1,), (1,)), ((), ())), preferred_element_type=jnp.float32
            ).astype(jnp.int32)


def fringe_picks(pick_ref, pick_rows, pick):
    pick_rows[...] = jnp.zeros(pick_rows.shape, jnp.int32)
    pick_rows[0:1, 0 : pick_ref.shape[1]] = pick_ref[...]
    row = lax.broadcasted_iota(jnp.int32, (8, LANES), 0)
    lane = lax.broadcasted_iota(jnp.int32, (8, LANES), 1)
    block, face = lane // 24, lane // 4 - 6 * (lane // 24)
    side, d = face // 3, face - 3 * (face // 3)
    t = jnp.minimum(8 * block + row, 24)
    number = ((2 * d + 1 - side) * 25 + t) * FRP + lane - 4 * (lane // 4)
    tile, place = number // LANES, number - LANES * (number // LANES)
    value = jnp.zeros((8, LANES), jnp.int32)
    for k in range(pick_rows.shape[1] // LANES):
        source = spread(pick_rows[0:1, k * LANES : (k + 1) * LANES], 8)
        value = jnp.where(tile == k, lane_take(source, place), value)
    pick[...] = value


def fringe_own(slot_ref, remote, own):
    lane = lax.broadcasted_iota(jnp.int32, (8, LANES), 1)
    for v in range(5):
        value = slot_ref[0, 0, v, 0:8, :]
        for k in range(6):
            for block in range(4):
                start = 24 * block + 4 * k
                source = slot_ref[k // 3, k % 3, v, 8 * block : 8 * block + 8, :]
                source = pltpu.roll(source, (start - remote) % LANES, axis=1)
                value = jnp.where((lane >= start) & (lane < start + 4), source, value)
        own[v] = value


def inner_jumps(remote, slot_ref, partner, scale_ref, inverse, jump):
    shared = lax.broadcasted_iota(jnp.int32, (ROWS, LANES), 1) < remote
    for d in range(3):
        high = [slot_ref[0, d, v] for v in range(5)]
        low = [slot_ref[1, d, v] for v in range(5)]

        def other(side, own):
            starts = [((side * 3 + d) * 5 + v) * ROWS for v in range(5)]
            return [jnp.where(shared, partner[s : s + ROWS, :], o) for s, o in zip(starts, own)]

        scale = spread(scale_ref[d : d + 1, :], ROWS)
        for side, value in (
            (0, common(high, other(1, low), d)),
            (1, common(other(0, high), low, d)),
        ):
            back = jnp.concatenate([inverse[side * 3 + d]] * 4, axis=0)
            start = (side * 3 + d) * ROWS
            for v in range(5):
                jump[v, start : start + ROWS, :] = lane_take(value[v], back) * scale


def fringe_jumps(remote, arrived_ref, pick, own, by_grid, scale_ref, inverse, jump, factor):
    parts, slots, width = arrived_ref.shape
    grids = by_grid.shape[0]
    each = parts * slots
    turned = arrived_ref[...].reshape(each, width)
    turned = jnp.concatenate([turned] * (LANES // each), axis=0).T
    by_grid[...] = turned[0 : grids * 8].reshape(grids, 8, LANES)
    chosen = pick[...]
    owner, place = chosen // each, chosen - each * (chosen // each)
    outside = [None] * 5
    for g in range(grids):
        for v in range(5):
            source = lane_take(spread(by_grid[g, v : v + 1, :], 8), place)
            outside[v] = source if g == 0 else jnp.where(owner == g, source, outside[v])
    inside = [own[v] for v in range(5)]
    lane = lax.broadcasted_iota(jnp.int32, (8, LANES), 1)
    face = lane // 4 - 6 * (lane // 24)
    d = face - 3 * (face // 3)
    normal = [d == n for n in range(3)]
    sign = jnp.where(face < 3, 0.5, -0.5)
    outer_flux, outer_wave = lane_euler(outside, normal)
    inner_flux, inner_wave = lane_euler(inside, normal)
    wave = sign * jnp.maximum(outer_wave, inner_wave)
    value = [
        0.5 * (a + b) - wave * (o - i)
        for a, b, o, i in zip(outer_flux, inner_flux, outside, inside)
    ]
    for v in range(5):
        for k in range(6):
            slot = inverse[k] - remote
            here = (slot >= 0) & (slot < FRP)
            slot = jnp.where(here, slot, 0) + 4 * k
            scale = spread(scale_ref[k % 3 : k % 3 + 1, :], 8)
            blocks = []
            for block in range(4):
                start = k * ROWS + 8 * block
                new = lane_take(value[v], slot + 24 * block) * scale
                blocks.append(jnp.where(here, new, jump[v, start : start + 8, :]))
            store_parts(factor, k * ROWS, v, jnp.concatenate(blocks, axis=0))


def ring_distance(offset, size):
    return min(offset, size - offset)


def kernel(grids, parts, *refs):
    inputs, (out_ref,), buffers, scratch = refs[:10], refs[10:11], refs[11:21], refs[21:]
    (state_ref, scale_ref, plus_ref, minus_ref, cell_ref, weight_ref, pick_ref) = buffers[:7]
    face_ref, volume_ref, lift_ref = buffers[7:]
    (
        points, donor, slot, message, partner_in, gathered, relay, arrived,
        face_factor, flux, lift_factor, total, inverse, pick_rows, pick, own, partner, jump, by_grid,
        load_sem, sends, recvs, entered,
    ) = scratch
    loads = [
        [
            pltpu.make_async_copy(source.at[v], target.at[v], load_sem.at[len(inputs) + v])
            for v in range(5)
        ]
        if n == 0
        else pltpu.make_async_copy(source, target, load_sem.at[n])
        for n, (source, target) in enumerate(zip(inputs, buffers))
    ]
    for copy in loads[0] + loads[4:6]:
        copy.start()
    grid = lax.axis_index("grid")
    part = lax.axis_index("dom")
    across, down = ACROSS, parts // ACROSS
    half = down // 2
    z, x = part // across, lax.rem(part, across)
    along_x = [lax.rem(x + k, across) for k in range(across)]
    along_grid = [lax.rem(grid + k, grids) for k in range(grids)]
    row_peers = [z * across + k for k in along_x[1:]]

    def for_lower(act):
        for k in range(down - 1, 0, -1):
            @pl.when(z >= k)
            def _(k=k):
                for column in along_x:
                    act((z - k) * across + column)

    def for_higher(act, low, high):
        for k in range(1, down):
            @pl.when((z + k >= low) & (z + k < high))
            def _(k=k):
                for column in along_x:
                    act((z + k) * across + column)

    barrier = pltpu.get_barrier_semaphore()

    def enter(peer):
        pl.semaphore_signal(barrier, inc=1, device_id=(grid, peer), device_id_type=MESH)

    for k in sorted(range(1, grids), key=lambda k: -ring_distance(k, grids)):
        pl.semaphore_signal(barrier, inc=1, device_id=(along_grid[k], part), device_id_type=MESH)
    for peer in row_peers:
        enter(peer)
    for_higher(enter, 0, down)
    for n in (2, 3, 7, 1, 6, 8, 9):
        loads[n].start()

    def send(n, source, place, target, mine, to_grid, to_part):
        pltpu.make_async_remote_copy(
            src_ref=source.at[place], dst_ref=target.at[mine],
            send_sem=sends.at[n], recv_sem=recvs.at[n],
            device_id=(to_grid, to_part), device_id_type=MESH,
        ).start()

    def finish(semaphore, buffer, count):
        whole = buffer.at[pl.ds(0, count)]
        pltpu.make_async_copy(whole, whole, semaphore).wait()

    mine = pl.ds(pl.multiple_of(part * 8, 8), 8)

    def told(peer):
        group = entered.at[z // max(half, 1)] if half else entered.at[0]
        pl.semaphore_signal(group, inc=1, device_id=(grid, peer), device_id_type=MESH)

    def send_faces(peer):
        send(1, message, pl.ds(pl.multiple_of(peer * 8, 8), 8), partner_in, mine, grid, peer)

    tiles = cell_ref.shape[-1] // LANES
    per_tile = grids // tiles
    near = grid // per_tile
    tile_steps = sorted(range(tiles), key=lambda k: -ring_distance(k, tiles))

    def make_tile(step):
        donor_tile(lax.rem(near + step, tiles), points, cell_ref, weight_ref, donor)

    def send_tile(step):
        first = lax.rem(grid, per_tile) + 1 if step == 0 else 0
        for k in range(per_tile if step else per_tile - 1):
            peer = lax.rem(near + step, tiles) * per_tile + lax.rem(first + k, per_tile)
            send(0, donor, peer, gathered, grid, peer, part)

    def make_faces():
        for n in (2, 3, 7):
            loads[n].wait()
        face_slots(points, plus_ref, minus_ref, face_ref, face_factor, slot)
        face_messages(slot, message)

    def pass_barrier():
        pl.semaphore_wait(barrier, grids - 1 + across * (z + 1) - 1)

    for copy in loads[0]:
        copy.wait()
    load_state(state_ref, points)
    loads[4].wait()
    loads[5].wait()

    late = (near == tiles // 2) | (near == tiles // 2 + 1)

    @pl.when(late)
    def _():
        for n, step in enumerate(tile_steps):
            make_tile(step)
            if n == 0:
                pass_barrier()
            send_tile(step)
            if n == 0:
                for_lower(told)
        make_faces()

    @pl.when(jnp.logical_not(late))
    def _():
        for step in tile_steps:
            make_tile(step)
        make_faces()
        pass_barrier()
        for step in tile_steps:
            send_tile(step)
        for_lower(told)

    for_lower(send_faces)
    for peer in row_peers:
        send_faces(peer)
    gathered[grid] = donor[grid]
    partner_in[mine, :] = message[mine, :]

    finish(recvs.at[0], gathered, grids - 1)
    turned = gathered[...].reshape(grids * 8, LANES)
    if grids * 8 < LANES:
        turned = jnp.concatenate([turned] * (LANES // (grids * 8)), axis=0)
    relay[...] = turned.T[0 : relay.shape[0] * relay.shape[1]].reshape(relay.shape)
    def send_donors(peer):
        send(2, relay, peer, arrived, part, grid, peer)

    def send_both(peer):
        send_donors(peer)
        send_faces(peer)

    for_lower(send_donors)
    for peer in row_peers:
        send_donors(peer)
    arrived[part] = relay[part]

    for n in (1, 6, 8, 9):
        loads[n].wait()
    volume_terms(points, scale_ref, volume_ref, flux, total)
    inverse_orders(plus_ref, minus_ref, inverse)
    fringe_picks(pick_ref, pick_rows, pick)
    fringe_own(slot, parts, own)
    for group, low, high in ((0, 0, half), (1, half, down)):
        later = across * jnp.maximum(high - jnp.maximum(z + 1, low), 0)

        @pl.when(later > 0)
        def _():
            pl.semaphore_wait(entered.at[group], later)
            for_higher(send_both, low, high)

    finish(recvs.at[1], partner_in, 8 * (parts - 1))
    partner_faces(partner_in, partner)
    inner_jumps(parts, slot, partner, scale_ref, inverse, jump)
    finish(sends.at[0], donor, grids - 1)
    finish(sends.at[1], message, 8 * (parts - 1))
    finish(sends.at[2], relay, parts - 1)

    finish(recvs.at[2], arrived, parts - 1)
    fringe_jumps(parts, arrived, pick, own, by_grid, scale_ref, inverse, jump, lift_factor)
    for v, value in products(lift_ref, lift_factor):
        out_ref[v] = (total[v] + value)[0:125]


def body(grids, parts, state, scales, plus, minus, cell, weights, picks):
    f32, i32 = jnp.float32, jnp.int32
    total_slots = cell.shape[-1]
    slots = total_slots // (grids * parts)
    weights = jnp.transpose(weights, (1, 2, 0, 3))
    inputs = (state, scales, plus, minus, cell, weights, picks) + matrices()
    pick_tiles = -(-picks.shape[-1] // LANES)
    return pl.pallas_call(
        functools.partial(kernel, grids, parts),
        out_shape=jax.ShapeDtypeStruct(state.shape, f32),
        in_specs=[pl.BlockSpec(memory_space=pltpu.HBM)] * len(inputs),
        out_specs=pl.BlockSpec(memory_space=pltpu.VMEM),
        scratch_shapes=[pltpu.VMEM(x.shape, x.dtype) for x in inputs]
        + [
            pltpu.VMEM((5, LANES, LANES), f32),
            pltpu.VMEM((grids, 8, LANES), f32),
            pltpu.VMEM((2, 3, 5, ROWS, LANES), f32),
            pltpu.VMEM((parts * 8, LANES), f32),
            pltpu.VMEM((parts * 8, LANES), f32),
            pltpu.VMEM((grids, 8, LANES), f32),
            pltpu.VMEM((parts, slots, LANES), f32),
            pltpu.VMEM((parts, slots, LANES), f32),
            pltpu.VMEM((3 * LANES, 5 * LANES), jnp.bfloat16),
            pltpu.VMEM((9 * LANES, 5 * LANES), jnp.bfloat16),
            pltpu.VMEM((18 * ROWS, 5 * LANES), jnp.bfloat16),
            pltpu.VMEM((5, LANES, LANES), f32),
            pltpu.VMEM((6, 8, LANES), i32),
            pltpu.VMEM((8, pick_tiles * LANES), i32),
            pltpu.VMEM((8, LANES), i32),
            pltpu.VMEM((5, 8, LANES), f32),
            pltpu.VMEM((8 * LANES, LANES), f32),
            pltpu.VMEM((5, 6 * ROWS, LANES), f32),
            pltpu.VMEM((grids, 8, LANES), f32),
            pltpu.SemaphoreType.DMA((len(inputs) + 5,)),
            pltpu.SemaphoreType.DMA((3,)),
            pltpu.SemaphoreType.DMA((3,)),
            pltpu.SemaphoreType.REGULAR((2,)),
        ],
        compiler_params=pltpu.CompilerParams(
            collective_id=0, has_side_effects=True, vmem_limit_bytes=24 * 1024 * 1024
        ),
        name="step",
    )(*(pltpu.with_memory_space_constraint(x, pltpu.HBM) for x in inputs))


def solution(mesh):
    both = ("grid", "dom")
    return jax.shard_map(
        functools.partial(body, mesh.shape["grid"], mesh.shape["dom"]),
        mesh=mesh,
        in_specs=(
            P(None, None, both),
            P(None, both),
            P(None, both),
            P(None, both),
            P(both, None),
            P(both, None, None, None),
            P(both, None),
        ),
        out_specs=P(None, None, both),
        check_vma=False,
    )
```

```python
import functools
import math

import jax
import jax.numpy as jnp
import numpy as np
from jax import lax
from jax.experimental import pallas as pl
from jax.experimental.pallas import tpu as pltpu
from jax.sharding import PartitionSpec as P

MESH = pl.DeviceIdType.MESH
LANES = 128
ROWS = 32
FRP = 4
ACROSS = 4


def gauss_nodes():
    outer = math.sqrt(5.0 + 2.0 * math.sqrt(10.0 / 7.0)) / 3.0
    inner = math.sqrt(5.0 - 2.0 * math.sqrt(10.0 / 7.0)) / 3.0
    return [-outer, -inner, 0.0, inner, outer]


def basis_value(nodes, column, x):
    value = 1.0
    for other in range(5):
        if other != column:
            value = value * (x - nodes[other]) / (nodes[column] - nodes[other])
    return value


def basis_slope(nodes, column, x):
    total = 0.0
    for skipped in range(5):
        if skipped != column:
            value = 1.0 / (nodes[column] - nodes[skipped])
            for other in range(5):
                if other != column and other != skipped:
                    value = value * (x - nodes[other]) / (nodes[column] - nodes[other])
            total = total + value
    return total


def legendre_slopes(x):
    values = [1.0, x]
    slopes = [0.0, 1.0]
    for order in range(1, 5):
        values.append(((2 * order + 1) * x * values[order] - order * values[order - 1]) / (order + 1))
        slopes.append(slopes[order - 1] + (2 * order + 1) * values[order])
    return slopes[4], slopes[5]


def split_point(p, direction):
    index = [p // 25, p // 5 % 5, p % 5]
    along = index.pop(direction)
    return along, 5 * index[0] + index[1]


def split_constant(matrix):
    high = matrix.astype(jnp.bfloat16)
    low = (matrix - high.astype(np.float32)).astype(jnp.bfloat16)
    return jnp.asarray(np.concatenate([high, high, low], axis=1))


def matrices():
    nodes = gauss_nodes()
    deriv = np.array([[basis_slope(nodes, m, x) for m in range(5)] for x in nodes])
    lower = np.array([basis_value(nodes, m, -1.0) for m in range(5)])
    upper = np.array([basis_value(nodes, m, 1.0) for m in range(5)])
    slopes = [legendre_slopes(x) for x in nodes]
    lift_low = np.array([-0.5 * (five - four) for four, five in slopes])
    lift_high = np.array([0.5 * (five + four) for four, five in slopes])
    folded = deriv - np.outer(lift_low, lower) - np.outer(lift_high, upper)
    faces = np.zeros((2, 3, ROWS, LANES))
    volume = np.zeros((LANES, 3, LANES))
    lift = np.zeros((LANES, 2, 3, ROWS))
    for direction in range(3):
        for p in range(125):
            i, t = split_point(p, direction)
            faces[0, direction, t, p] = upper[i]
            faces[1, direction, t, p] = lower[i]
            lift[p, 0, direction, t] = -lift_high[i]
            lift[p, 1, direction, t] = -lift_low[i]
            for other in range(125):
                m, s = split_point(other, direction)
                if s == t:
                    volume[p, direction, other] = -folded[i, m]
    faces[:, :, 25:] = faces[:, :, :1]
    return tuple(
        split_constant(m.astype(np.float32))
        for m in (
            faces.reshape(6 * ROWS, LANES),
            volume.reshape(LANES, 3 * LANES),
            lift.reshape(LANES, 6 * ROWS),
        )
    )


def lane_take(x, index):
    return jnp.take_along_axis(x, index, axis=1, mode="promise_in_bounds")


def spread(row, rows):
    return jnp.broadcast_to(row, (rows, row.shape[-1]))


def store_parts(ref, start, v, value):
    third = ref.shape[0] // 3
    rows, lanes = value.shape[0], slice(v * LANES, (v + 1) * LANES)
    high = value.astype(jnp.bfloat16)
    ref[start : start + rows, lanes] = high
    ref[third + start : third + start + rows, lanes] = (value - high.astype(jnp.float32)).astype(jnp.bfloat16)
    ref[2 * third + start : 2 * third + start + rows, lanes] = high


def products(constant_ref, ref):
    for v in range(0, 5, 2):
        width = min(2, 5 - v) * LANES
        block = jnp.dot(
            constant_ref[...], ref[:, v * LANES : v * LANES + width], preferred_element_type=jnp.float32
        )
        for k in range(width // LANES):
            yield v + k, block[:, k * LANES : (k + 1) * LANES]


def pressure_of(w, inverse):
    square = w[1] * w[1] + w[2] * w[2] + w[3] * w[3]
    return 0.4 * (w[4] - 0.5 * square * inverse)


def euler(w, direction):
    inverse = 1.0 / w[0]
    speed = w[1 + direction] * inverse
    pressure = pressure_of(w, inverse)
    flux = [w[1 + direction]] + [m * speed for m in w[1:4]] + [(w[4] + pressure) * speed]
    flux[1 + direction] = flux[1 + direction] + (pressure - 1.0)
    return flux, jnp.abs(speed) + jnp.sqrt(1.4 * pressure * inverse)


def common(left, right, direction):
    left_flux, left_wave = euler(left, direction)
    right_flux, right_wave = euler(right, direction)
    wave = jnp.maximum(left_wave, right_wave)
    return [
        0.5 * (lf + rf) - 0.5 * wave * (r - l)
        for lf, rf, l, r in zip(left_flux, right_flux, left, right)
    ]


def lane_euler(w, normal):
    inverse = 1.0 / w[0]
    momentum = jnp.where(normal[0], w[1], jnp.where(normal[1], w[2], w[3]))
    speed = momentum * inverse
    pressure = pressure_of(w, inverse)
    flux = [momentum] + [
        w[1 + d] * speed + jnp.where(normal[d], pressure - 1.0, 0.0) for d in range(3)
    ]
    flux.append((w[4] + pressure) * speed)
    return flux, jnp.abs(speed) + jnp.sqrt(1.4 * pressure * inverse)


def load_state(state_ref, points):
    for v in range(5):
        points[v, 0:120, :] = state_ref[v, 0:120, :]
        points[v, 120:125, :] = state_ref[v, 120:125, :]
        points[v, 125:128, :] = state_ref[v, 122:125, :]


def row_choice(row, values, index):
    value = values[index[-1]]
    for s in range(len(index) - 2, -1, -1):
        if index[s] != index[s + 1]:
            value = jnp.where(row <= s, values[index[s]], value)
    return value


def donor_tile(tile, points, cell_ref, weight_ref, donor_ref):
    per_tile = LANES * donor_ref.shape[0] // cell_ref.shape[-1]
    lanes = pl.ds(pl.multiple_of(tile * LANES, LANES), LANES)
    row = lax.broadcasted_iota(jnp.int32, (8, LANES), 0)
    turn = row - 5 * (row // 5)
    along = [[spread(weight_ref[d, k, :, lanes], 8) for k in range(5)] for d in range(3)]
    last = []
    for start in range(5):
        value = along[2][(start + 4) % 5]
        for k in range(4):
            value = jnp.where(turn == k, along[2][(start + k) % 5], value)
        last.append(value)
    index = spread(cell_ref[0:1, lanes], 8)
    sums = [None] * 5
    for k in range(LANES // 8):
        number = [min(8 * k + s, 124) for s in range(8)]
        scale = row_choice(row, along[0], [p // 25 for p in number])
        pairs = [p // 5 for p in number]
        middle = row_choice(row, [along[1][p % 5] for p in range(25)], pairs)
        scale = scale * middle * last[8 * k % 5]
        if 8 * k + 8 > 125:
            scale = jnp.where(row < 125 - 8 * k, scale, 0.0)
        for v in range(5):
            term = lane_take(points[v, 8 * k : 8 * k + 8, :], index) * scale
            sums[v] = term if k == 0 else sums[v] + term
    value = jnp.zeros((8, LANES), jnp.float32)
    for v in range(5):
        value = jnp.where(row == v, jnp.sum(sums[v], axis=0, keepdims=True), value)
    donor_ref[tile * per_tile] = value
    for k in range(1, per_tile):
        donor_ref[tile * per_tile + k] = pltpu.roll(value, LANES - k * (LANES // per_tile), axis=1)


def face_slots(points, plus_ref, minus_ref, face_ref, factor, slot_ref):
    centre = (1.0, 0.0, 0.0, 0.0, 2.5)
    for v in range(5):
        store_parts(factor, 0, v, points[v] - centre[v])
    for v, faces in products(face_ref, factor):
        for side, order in ((0, plus_ref), (1, minus_ref)):
            for d in range(3):
                start = (side * 3 + d) * ROWS
                slot_ref[side, d, v] = centre[v] + lane_take(
                    faces[start : start + ROWS], spread(order[d : d + 1, :], ROWS)
                )


def face_messages(slot_ref, message_ref):
    count = message_ref.shape[0] // 8
    for row in range(8):
        columns = [
            slot_ref[n // 15, n // 5 % 3, n % 5] for n in range(4 * row, min(4 * row + 4, 30))
        ]
        columns += [columns[-1]] * (4 - len(columns))
        message_ref[pl.ds(row, count, stride=8), :] = jnp.concatenate(columns, axis=0).T[0:count]


def partner_faces(partner_in, partner):
    count = partner_in.shape[0] // 8
    for row in range(8):
        block = partner_in[pl.ds(row, count, stride=8), :]
        block = jnp.concatenate([block] * (LANES // count), axis=0).T
        partner[row * LANES : (row + 1) * LANES, :] = block


def volume_terms(points, scale_ref, volume_ref, flux, total):
    w = [points[v] for v in range(5)]
    for d in range(3):
        pieces = euler(w, d)[0]
        for v in range(5):
            store_parts(flux, d * LANES, v, pieces[v] * spread(scale_ref[d : d + 1, :], LANES))
    for v, value in products(volume_ref, flux):
        total[v] = value


def inverse_orders(plus_ref, minus_ref, inverse):
    element = lax.broadcasted_iota(jnp.int32, (LANES, LANES), 0)
    count = lax.broadcasted_iota(jnp.int32, (8, LANES), 1).astype(jnp.float32).astype(jnp.bfloat16)
    for side, order in ((0, plus_ref), (1, minus_ref)):
        for d in range(3):
            chosen = element == spread(order[d : d + 1, :], LANES)
            chosen = jnp.where(chosen, 1.0, 0.0).astype(jnp.bfloat16)
            inverse[side * 3 + d] = lax.dot_general(
                count, chosen, (((1,), (1,)), ((), ())), preferred_element_type=jnp.float32
            ).astype(jnp.int32)


def fringe_picks(pick_ref, pick_rows, pick):
    pick_rows[...] = jnp.zeros(pick_rows.shape, jnp.int32)
    pick_rows[0:1, 0 : pick_ref.shape[1]] = pick_ref[...]
    row = lax.broadcasted_iota(jnp.int32, (8, LANES), 0)
    lane = lax.broadcasted_iota(jnp.int32, (8, LANES), 1)
    block, face = lane // 24, lane // 4 - 6 * (lane // 24)
    side, d = face // 3, face - 3 * (face // 3)
    t = jnp.minimum(8 * block + row, 24)
    number = ((2 * d + 1 - side) * 25 + t) * FRP + lane - 4 * (lane // 4)
    tile, place = number // LANES, number - LANES * (number // LANES)
    value = jnp.zeros((8, LANES), jnp.int32)
    for k in range(pick_rows.shape[1] // LANES):
        source = spread(pick_rows[0:1, k * LANES : (k + 1) * LANES], 8)
        value = jnp.where(tile == k, lane_take(source, place), value)
    pick[...] = value


def fringe_own(slot_ref, remote, own):
    lane = lax.broadcasted_iota(jnp.int32, (8, LANES), 1)
    for v in range(5):
        value = slot_ref[0, 0, v, 0:8, :]
        for k in range(6):
            for block in range(4):
                start = 24 * block + 4 * k
                source = slot_ref[k // 3, k % 3, v, 8 * block : 8 * block + 8, :]
                source = pltpu.roll(source, (start - remote) % LANES, axis=1)
                value = jnp.where((lane >= start) & (lane < start + 4), source, value)
        own[v] = value


def inner_jumps(remote, slot_ref, partner, scale_ref, inverse, jump):
    shared = lax.broadcasted_iota(jnp.int32, (ROWS, LANES), 1) < remote
    for d in range(3):
        high = [slot_ref[0, d, v] for v in range(5)]
        low = [slot_ref[1, d, v] for v in range(5)]

        def other(side, own):
            starts = [((side * 3 + d) * 5 + v) * ROWS for v in range(5)]
            return [jnp.where(shared, partner[s : s + ROWS, :], o) for s, o in zip(starts, own)]

        scale = spread(scale_ref[d : d + 1, :], ROWS)
        for side, value in (
            (0, common(high, other(1, low), d)),
            (1, common(other(0, high), low, d)),
        ):
            back = jnp.concatenate([inverse[side * 3 + d]] * 4, axis=0)
            start = (side * 3 + d) * ROWS
            for v in range(5):
                jump[v, start : start + ROWS, :] = lane_take(value[v], back) * scale


def fringe_jumps(remote, arrived_ref, pick, own, by_grid, scale_ref, inverse, jump, factor):
    parts, slots, width = arrived_ref.shape
    grids = by_grid.shape[0]
    each = parts * slots
    turned = arrived_ref[...].reshape(each, width)
    turned = jnp.concatenate([turned] * (LANES // each), axis=0).T
    by_grid[...] = turned[0 : grids * 8].reshape(grids, 8, LANES)
    chosen = pick[...]
    owner, place = chosen // each, chosen - each * (chosen // each)
    outside = [None] * 5
    for g in range(grids):
        for v in range(5):
            source = lane_take(spread(by_grid[g, v : v + 1, :], 8), place)
            outside[v] = source if g == 0 else jnp.where(owner == g, source, outside[v])
    inside = [own[v] for v in range(5)]
    lane = lax.broadcasted_iota(jnp.int32, (8, LANES), 1)
    face = lane // 4 - 6 * (lane // 24)
    d = face - 3 * (face // 3)
    normal = [d == n for n in range(3)]
    sign = jnp.where(face < 3, 0.5, -0.5)
    outer_flux, outer_wave = lane_euler(outside, normal)
    inner_flux, inner_wave = lane_euler(inside, normal)
    wave = sign * jnp.maximum(outer_wave, inner_wave)
    value = [
        0.5 * (a + b) - wave * (o - i)
        for a, b, o, i in zip(outer_flux, inner_flux, outside, inside)
    ]
    for v in range(5):
        for k in range(6):
            slot = inverse[k] - remote
            here = (slot >= 0) & (slot < FRP)
            slot = jnp.where(here, slot, 0) + 4 * k
            scale = spread(scale_ref[k % 3 : k % 3 + 1, :], 8)
            blocks = []
            for block in range(4):
                start = k * ROWS + 8 * block
                new = lane_take(value[v], slot + 24 * block) * scale
                blocks.append(jnp.where(here, new, jump[v, start : start + 8, :]))
            store_parts(factor, k * ROWS, v, jnp.concatenate(blocks, axis=0))


def ring_distance(offset, size):
    return min(offset, size - offset)


def kernel(grids, parts, *refs):
    inputs, (out_ref,), buffers, scratch = refs[:10], refs[10:11], refs[11:21], refs[21:]
    (state_ref, scale_ref, plus_ref, minus_ref, cell_ref, weight_ref, pick_ref) = buffers[:7]
    face_ref, volume_ref, lift_ref = buffers[7:]
    (
        points, donor, slot, message, partner_in, gathered, relay, arrived,
        face_factor, flux, lift_factor, total, inverse, pick_rows, pick, own, partner, jump, by_grid,
        load_sem, sends, recvs, entered,
    ) = scratch
    loads = [
        [
            pltpu.make_async_copy(source.at[v], target.at[v], load_sem.at[len(inputs) + v])
            for v in range(5)
        ]
        if n == 0
        else pltpu.make_async_copy(source, target, load_sem.at[n])
        for n, (source, target) in enumerate(zip(inputs, buffers))
    ]
    for copy in loads[0] + loads[4:6]:
        copy.start()
    grid = lax.axis_index("grid")
    part = lax.axis_index("dom")
    across, down = ACROSS, parts // ACROSS
    half = down // 2
    z, x = part // across, lax.rem(part, across)
    along_x = [lax.rem(x + k, across) for k in range(across)]
    along_grid = [lax.rem(grid + k, grids) for k in range(grids)]
    row_peers = [z * across + k for k in along_x[1:]]

    def for_lower(act):
        for k in range(down - 1, 0, -1):
            @pl.when(z >= k)
            def _(k=k):
                for column in along_x:
                    act((z - k) * across + column)

    def for_higher(act, low, high):
        for k in range(1, down):
            @pl.when((z + k >= low) & (z + k < high))
            def _(k=k):
                for column in along_x:
                    act((z + k) * across + column)

    barrier = pltpu.get_barrier_semaphore()

    def enter(peer):
        pl.semaphore_signal(barrier, inc=1, device_id=(grid, peer), device_id_type=MESH)

    for k in sorted(range(1, grids), key=lambda k: -ring_distance(k, grids)):
        pl.semaphore_signal(barrier, inc=1, device_id=(along_grid[k], part), device_id_type=MESH)
    for peer in row_peers:
        enter(peer)
    for_higher(enter, 0, down)
    for n in (2, 3, 7, 1, 6, 8, 9):
        loads[n].start()

    def send(n, source, place, target, mine, to_grid, to_part):
        pltpu.make_async_remote_copy(
            src_ref=source.at[place], dst_ref=target.at[mine],
            send_sem=sends.at[n], recv_sem=recvs.at[n],
            device_id=(to_grid, to_part), device_id_type=MESH,
        ).start()

    def finish(semaphore, buffer, count):
        whole = buffer.at[pl.ds(0, count)]
        pltpu.make_async_copy(whole, whole, semaphore).wait()

    mine = pl.ds(pl.multiple_of(part * 8, 8), 8)

    def told(peer):
        group = entered.at[z // max(half, 1)] if half else entered.at[0]
        pl.semaphore_signal(group, inc=1, device_id=(grid, peer), device_id_type=MESH)

    def send_faces(peer):
        send(1, message, pl.ds(pl.multiple_of(peer * 8, 8), 8), partner_in, mine, grid, peer)

    tiles = cell_ref.shape[-1] // LANES
    per_tile = grids // tiles
    near = grid // per_tile
    tile_steps = sorted(range(tiles), key=lambda k: -ring_distance(k, tiles))

    def make_tile(step):
        donor_tile(lax.rem(near + step, tiles), points, cell_ref, weight_ref, donor)

    def send_tile(step):
        first = lax.rem(grid, per_tile) + 1 if step == 0 else 0
        for k in range(per_tile if step else per_tile - 1):
            peer = lax.rem(near + step, tiles) * per_tile + lax.rem(first + k, per_tile)
            send(0, donor, peer, gathered, grid, peer, part)

    def make_faces():
        for n in (2, 3, 7):
            loads[n].wait()
        face_slots(points, plus_ref, minus_ref, face_ref, face_factor, slot)
        face_messages(slot, message)

    def pass_barrier():
        pl.semaphore_wait(barrier, grids - 1 + across * (z + 1) - 1)

    for copy in loads[0]:
        copy.wait()
    load_state(state_ref, points)
    loads[4].wait()
    loads[5].wait()

    late = (near >= tiles // 2) & (near <= tiles // 2 + 2)

    @pl.when(late)
    def _():
        for n, step in enumerate(tile_steps):
            make_tile(step)
            if n == 0:
                pass_barrier()
            send_tile(step)
            if n == 0:
                for_lower(told)
        make_faces()

    @pl.when(jnp.logical_not(late))
    def _():
        for step in tile_steps:
            make_tile(step)
        make_faces()
        pass_barrier()
        for step in tile_steps:
            send_tile(step)
        for_lower(told)

    for_lower(send_faces)
    for peer in row_peers:
        send_faces(peer)
    gathered[grid] = donor[grid]
    partner_in[mine, :] = message[mine, :]

    finish(recvs.at[0], gathered, grids - 1)
    turned = gathered[...].reshape(grids * 8, LANES)
    if grids * 8 < LANES:
        turned = jnp.concatenate([turned] * (LANES // (grids * 8)), axis=0)
    relay[...] = turned.T[0 : relay.shape[0] * relay.shape[1]].reshape(relay.shape)
    def send_donors(peer):
        send(2, relay, peer, arrived, part, grid, peer)

    def send_both(peer):
        send_donors(peer)
        send_faces(peer)

    for_lower(send_donors)
    for peer in row_peers:
        send_donors(peer)
    arrived[part] = relay[part]

    for n in (1, 6, 8, 9):
        loads[n].wait()
    volume_terms(points, scale_ref, volume_ref, flux, total)
    inverse_orders(plus_ref, minus_ref, inverse)
    fringe_picks(pick_ref, pick_rows, pick)
    fringe_own(slot, parts, own)
    for group, low, high in ((0, 0, half), (1, half, down)):
        later = across * jnp.maximum(high - jnp.maximum(z + 1, low), 0)

        @pl.when(later > 0)
        def _():
            pl.semaphore_wait(entered.at[group], later)
            for_higher(send_both, low, high)

    finish(recvs.at[1], partner_in, 8 * (parts - 1))
    partner_faces(partner_in, partner)
    inner_jumps(parts, slot, partner, scale_ref, inverse, jump)
    finish(sends.at[0], donor, grids - 1)
    finish(sends.at[1], message, 8 * (parts - 1))
    finish(sends.at[2], relay, parts - 1)

    finish(recvs.at[2], arrived, parts - 1)
    fringe_jumps(parts, arrived, pick, own, by_grid, scale_ref, inverse, jump, lift_factor)
    for v, value in products(lift_ref, lift_factor):
        out_ref[v] = (total[v] + value)[0:125]


def body(grids, parts, state, scales, plus, minus, cell, weights, picks):
    f32, i32 = jnp.float32, jnp.int32
    total_slots = cell.shape[-1]
    slots = total_slots // (grids * parts)
    weights = jnp.transpose(weights, (1, 2, 0, 3))
    inputs = (state, scales, plus, minus, cell, weights, picks) + matrices()
    pick_tiles = -(-picks.shape[-1] // LANES)
    return pl.pallas_call(
        functools.partial(kernel, grids, parts),
        out_shape=jax.ShapeDtypeStruct(state.shape, f32),
        in_specs=[pl.BlockSpec(memory_space=pltpu.HBM)] * len(inputs),
        out_specs=pl.BlockSpec(memory_space=pltpu.VMEM),
        scratch_shapes=[pltpu.VMEM(x.shape, x.dtype) for x in inputs]
        + [
            pltpu.VMEM((5, LANES, LANES), f32),
            pltpu.VMEM((grids, 8, LANES), f32),
            pltpu.VMEM((2, 3, 5, ROWS, LANES), f32),
            pltpu.VMEM((parts * 8, LANES), f32),
            pltpu.VMEM((parts * 8, LANES), f32),
            pltpu.VMEM((grids, 8, LANES), f32),
            pltpu.VMEM((parts, slots, LANES), f32),
            pltpu.VMEM((parts, slots, LANES), f32),
            pltpu.VMEM((3 * LANES, 5 * LANES), jnp.bfloat16),
            pltpu.VMEM((9 * LANES, 5 * LANES), jnp.bfloat16),
            pltpu.VMEM((18 * ROWS, 5 * LANES), jnp.bfloat16),
            pltpu.VMEM((5, LANES, LANES), f32),
            pltpu.VMEM((6, 8, LANES), i32),
            pltpu.VMEM((8, pick_tiles * LANES), i32),
            pltpu.VMEM((8, LANES), i32),
            pltpu.VMEM((5, 8, LANES), f32),
            pltpu.VMEM((8 * LANES, LANES), f32),
            pltpu.VMEM((5, 6 * ROWS, LANES), f32),
            pltpu.VMEM((grids, 8, LANES), f32),
            pltpu.SemaphoreType.DMA((len(inputs) + 5,)),
            pltpu.SemaphoreType.DMA((3,)),
            pltpu.SemaphoreType.DMA((3,)),
            pltpu.SemaphoreType.REGULAR((2,)),
        ],
        compiler_params=pltpu.CompilerParams(
            collective_id=0, has_side_effects=True, vmem_limit_bytes=24 * 1024 * 1024
        ),
        name="step",
    )(*(pltpu.with_memory_space_constraint(x, pltpu.HBM) for x in inputs))


def solution(mesh):
    both = ("grid", "dom")
    return jax.shard_map(
        functools.partial(body, mesh.shape["grid"], mesh.shape["dom"]),
        mesh=mesh,
        in_specs=(
            P(None, None, both),
            P(None, both),
            P(None, both),
            P(None, both),
            P(both, None),
            P(both, None, None, None),
            P(both, None),
        ),
        out_specs=P(None, None, both),
        check_vma=False,
    )
```
